32 devices in a mesh: grp: 4 (over y, x), blk: 8 (over z, core).
Axes of the slice: x: 2, y: 2, z: 4, core: 2. Of those that a mesh axis runs over, the one named last changes fastest.
Arguments:
- activations: bfloat16 [32768, 3072], P(('grp', 'blk')), may hold values from -6 to 6
- out_grads: bfloat16 [32768, 3072], P(('grp', 'blk')), may hold values from -6 to 6
- proj_act: bfloat16 [3072, 128], replicated, may hold values from -1 to 1
- proj_out: bfloat16 [3072, 256], replicated, may hold values from -0.109375 to 0.109375
Outputs:
- scores: float32 [512, 128], P(('grp', 'blk'))
The draws below stay inside these ranges and needn't reach their ends.
All inputs are finite; a program needn't handle non-finite values.
Results may differ from the reference program's by a relative error of at most 0.0012.
Values may be sent and summed in bfloat16 or wider, within the bound.
A program may use at most 128 MiB of HBM per device.

```python
import math
import jax
import jax.numpy as jnp
from jax import lax

D = 3072
RA = 128
RB = 256
SEQ = 64
ITERS = 4
EX_DEV = 16
GROUPS = 4
BLOCKS = 8
GROUP_EX = 128
EXAMPLES = 512
TOKENS = 32768
COORDS = 32768
COORD_BLK = 4096


def draw_proj_act(key, part):
    base = jnp.clip(jax.random.normal(jax.random.fold_in(key, 11), (D, RA), jnp.float32), -6.0, 6.0)
    ladder = jnp.arange(RA).astype(jnp.float32) / RA
    jitter = jax.random.uniform(jax.random.fold_in(key, 12), (RA,), jnp.float32, -0.4, 0.4)
    column = jnp.exp(ladder * math.log(3.0) + jitter)
    values = jnp.clip(base * column / math.sqrt(D), -1.0, 1.0)
    return values.astype(jnp.bfloat16)


def level_of(key, shape, pieces, smallest, top_value):
    def one(axis_at, blocks):
        steps = jax.random.uniform(jax.random.fold_in(jax.random.fold_in(key, 6), axis_at), (blocks,), jnp.float32, smallest / len(pieces), top_value / len(pieces))
        return jnp.repeat(jnp.exp(steps), shape[axis_at] // blocks).reshape((-1,) + (1,) * (len(shape) - axis_at - 1))

    loudness = one(*pieces[0])
    for cut in pieces[1:]:
        loudness = loudness * one(*cut)
    return loudness


def normal_values(own_key, shape, deviation, limit, cuts=(), held_as=jnp.bfloat16):
    values = jax.random.normal(own_key, shape, jnp.float32) * deviation
    if len(cuts) > 0:
        values = level_of(own_key, shape, cuts, -0.22, 0.18) * values
    return jnp.clip(values, min=-limit, max=limit).astype(held_as)


def setup_inputs(seed: int = 0) -> dict:
    splits = jax.random.split(jax.random.key(seed), 5)
    return {
        "activations": normal_values(splits[0], (TOKENS, D), 1.0, 6.0, ((0, 32),)),
        "out_grads": normal_values(splits[1], (TOKENS, D), 1.0, 6.0, ((0, 32),)),
        "proj_act": draw_proj_act(jax.random.fold_in(splits[4], 71), 0),
        "proj_out": normal_values(splits[3], (D, RB), D ** -0.5, 0.109375),
    }


damping_rate = 0.5
power_steps = 3

def top_estimate(gram_sum):
    width = gram_sum.shape[0]
    vector = jnp.full((width,), 1.0 / math.sqrt(width), jnp.float32)
    top = jnp.float32(1.0)
    for step in range(power_steps):
        image = jnp.dot(gram_sum, vector, precision=lax.Precision.HIGHEST)
        top = jnp.sqrt(jnp.sum(image * image) + 1e-06)
        vector = image / top
    return top

def chebyshev(gram_sum, damping, right_side):
    radius = top_estimate(gram_sum)
    center = damping + radius

    def operate(field):
        return jnp.dot(gram_sum, field, precision=lax.Precision.HIGHEST) + damping * field
    stride = 1.0 / center
    direction = right_side
    solution = stride * direction
    residual = right_side - stride * operate(direction)
    for sweep in range(1, ITERS):
        if sweep == 1:
            momentum = 0.5 * (radius * stride) ** 2
        else:
            momentum = (0.5 * radius * stride) ** 2
        stride = 1.0 / (center - momentum / stride)
        direction = residual + momentum * direction
        solution = solution + stride * direction
        if sweep + 1 < ITERS:
            residual = residual - stride * operate(direction)
    return solution

def reference(activations, out_grads, proj_act, proj_out):
    act_low = jnp.dot(activations, proj_act, preferred_element_type=jnp.float32).astype(jnp.bfloat16)
    grad_low = jnp.dot(out_grads, proj_out, preferred_element_type=jnp.float32).astype(jnp.bfloat16)
    features = jnp.einsum('etr,ets->ers', act_low.reshape(EXAMPLES, SEQ, RA).astype(jnp.float32), grad_low.reshape(EXAMPLES, SEQ, RB).astype(jnp.float32), precision=lax.Precision.HIGHEST)
    features = features.astype(jnp.bfloat16).reshape(EXAMPLES, COORDS)
    widened = features.astype(jnp.float32)
    total = jnp.sum(widened * widened)
    damping = damping_rate * total / COORDS
    grouped = features.reshape(GROUPS, GROUP_EX, BLOCKS, COORD_BLK)

    def one_block(running, block_rows):
        wide_rows = block_rows.astype(jnp.float32)
        gram_sum = jnp.einsum('gec,ged->cd', wide_rows, wide_rows, precision=lax.Precision.HIGHEST)

        def per_group(rows):
            solved = chebyshev(gram_sum, damping, rows.T)
            solved = lax.optimization_barrier(solved.astype(jnp.bfloat16)).astype(jnp.float32)
            return jnp.dot(rows, solved, precision=lax.Precision.HIGHEST)
        return (running + jax.vmap(per_group)(wide_rows), None)
    start_sum = jnp.zeros((GROUPS, GROUP_EX, GROUP_EX), jnp.float32)
    running, _ = lax.scan(one_block, start_sum, jnp.moveaxis(grouped, 2, 0))
    return running.reshape(EXAMPLES, GROUP_EX) * float(EX_DEV * GROUPS)
```

```python
import functools
import math

import jax
import jax.numpy as jnp
from jax import lax
from jax.experimental import pallas as pl
from jax.experimental.pallas import tpu as pltpu
from jax.sharding import PartitionSpec as P

SEQ = 64
ITERS = 4
damping_rate = 0.5
power_steps = 3
CHUNKS = 2
PARTS = 4
UNITS = 4
MESH = pl.DeviceIdType.MESH
NT = (((1,), (1,)), ((), ()))
TN = (((0,), (0,)), ((), ()))
TILES = [(i, j) for i in range(UNITS) for j in range(i + 1)]


def mix_kernel(
    groups, blocks, examples, ranks, width, slots,
    act_hbm, grad_hbm, pact_hbm, pout_hbm, out_ref,
    act_buf, grad_buf, pact, pout, wide, feat, recv, stat_acc, stat_row, stats_in, plane_row, stats_out,
    part, land1, land2, full, prow_part, prow_land, row, col, col_next, y_ref, pick, sc, sc_land,
    l_sem, w_sem, f_send, f_recv, a_send, a_recv, b_send, b_recv,
    s_send, s_recv, p_send, p_recv, o_send, o_recv,
):
    devices = groups * blocks
    planes = blocks // 2
    near = planes // 2
    cluster = 2 * groups
    group_ex = examples * blocks
    total_ex = group_ex * groups
    unit = total_ex // UNITS
    span = recv.shape[3]
    ex_c = examples // CHUNKS
    grp, blk = lax.axis_index("grp"), lax.axis_index("blk")
    core, plane = lax.rem(blk, 2), lax.div(blk, 2)
    side, row_of = lax.rem(grp, 2), lax.div(grp, 2)
    sign = 1 - 2 * lax.rem(plane, 2)
    solved = core * (groups // 2) + side

    def plane_at(rel):
        return lax.rem(plane + sign * rel + planes, planes)

    def seen_from(source, target):
        flip = 1 - 2 * lax.rem(target, 2)
        return lax.rem((source - target) * flip + planes, planes)

    def peer_of(d):
        rel = lax.rem(near + lax.div(d, cluster), planes)
        j = lax.rem(d, cluster)
        pg = lax.rem(grp + lax.div(j, 2), groups)
        pc = lax.rem(core + lax.rem(j, 2), 2)
        return pg, plane_at(rel), pc

    own = (planes - near) * cluster

    def over_peers(step):
        lax.fori_loop(0, own, step, 0)
        lax.fori_loop(own + 1, devices, step, 0)

    def over_plane(step):
        lax.fori_loop(own + 1, own + cluster, step, 0)

    barrier = pltpu.get_barrier_semaphore()

    def greet(d, c):
        pg, pp, pc = peer_of(d)
        pl.semaphore_signal(barrier, inc=1, device_id=(pg, 2 * pp + pc), device_id_type=MESH)
        return c

    rows_l = act_buf.shape[1]

    def load(k):
        at = pl.ds(k * rows_l, rows_l)
        return (
            pltpu.make_async_copy(act_hbm.at[at], act_buf.at[k % slots], l_sem.at[2 * (k % slots)]),
            pltpu.make_async_copy(grad_hbm.at[at], grad_buf.at[k % slots], l_sem.at[2 * (k % slots) + 1]),
        )

    load_pact = pltpu.make_async_copy(pact_hbm, pact, w_sem.at[0])
    load_pout = pltpu.make_async_copy(pout_hbm, pout, w_sem.at[1])
    load_pact.start()
    load(0)[0].start()
    load_pout.start()
    load(0)[1].start()
    for k in range(1, slots):
        for c in load(k):
            c.start()
    over_peers(greet)
    stat_acc[...] = jnp.zeros_like(stat_acc)

    per_part = rows_l // SEQ
    parts_c = PARTS // CHUNKS

    def project(k):
        first, second = load(k)
        if k == 0:
            load_pact.wait()
        first.wait()
        a_low = jnp.dot(
            act_buf[k % slots], pact[...], preferred_element_type=jnp.float32
        ).astype(jnp.bfloat16)
        if k == 0:
            load_pout.wait()
        second.wait()
        g_low = jnp.dot(
            grad_buf[k % slots], pout[...], preferred_element_type=jnp.float32
        ).astype(jnp.bfloat16)
        if k + slots < PARTS:
            for c in load(k + slots):
                c.start()
        for e in range(per_part):
            here = slice(e * SEQ, (e + 1) * SEQ)
            product = lax.dot_general(
                a_low[here], g_low[here], TN, preferred_element_type=jnp.float32)
            at = (k % parts_c) * per_part + e
            for h in range(wide.shape[0]):
                wide[h, pl.ds(at, a_low.shape[1], stride=ex_c), :] = (
                    product[:, h * 128:(h + 1) * 128])

    def rank_slot(pg, pp, pc):
        return (2 * pp + lax.div(pg, 2)) * groups + 2 * lax.rem(pg, 2) + pc

    def narrow(chunk, slot):
        for r in range(ranks):
            rows = pl.ds(pl.multiple_of((slot * ranks + r) * ex_c, ex_c), ex_c)
            for h in range(wide.shape[0]):
                low = wide[h, rows, :].astype(jnp.bfloat16)
                feat[chunk, slot, r, :, h * 128:(h + 1) * 128] = low
                back = low.astype(jnp.float32)
                stat_acc[...] += jnp.sum(
                    (back * back).reshape(ex_c // 8, 8, 128), axis=0)

    def landing(chunk, pp):
        rel = seen_from(plane, pp)
        u = 2 * lax.div(rel, near) + chunk
        at = (lax.rem(rel, near) * groups + grp) * 2 + core
        return recv.at[u, :, pl.ds(pl.multiple_of(at * ex_c, ex_c), ex_c), :], u

    def feature_copy(chunk, d):
        pg, pp, pc = peer_of(d)
        dst, u = landing(chunk, pp)
        return pltpu.make_async_remote_copy(
            src_ref=feat.at[chunk, rank_slot(pg, pp, pc)], dst_ref=dst,
            send_sem=f_send.at[chunk], recv_sem=f_recv.at[u],
            device_id=(pg, 2 * pp + pc), device_id_type=MESH)

    my_slot = rank_slot(grp, plane, core)

    for chunk in range(CHUNKS):
        for k in range(parts_c):
            project(chunk * parts_c + k)
        if chunk == 0:
            pl.semaphore_wait(barrier, devices - 1)

        def send(d, c, chunk=chunk):
            narrow(chunk, rank_slot(*peer_of(d)))
            feature_copy(chunk, d).start()
            return c

        over_peers(send)
        narrow(chunk, my_slot)
        dst, u = landing(chunk, plane)
        pltpu.make_async_copy(feat.at[chunk, my_slot], dst, f_recv.at[u]).start()

    def stat_in_copy(d):
        pg, pp, pc = peer_of(d)
        return pltpu.make_async_remote_copy(
            src_ref=stat_row, dst_ref=stats_in.at[d - own],
            send_sem=a_send.at[d - own], recv_sem=a_recv.at[d - own],
            device_id=(pg, 2 * pp + pc), device_id_type=MESH)

    def stat_out_copy(rel):
        slot = seen_from(plane, plane_at(rel))
        return pltpu.make_async_remote_copy(
            src_ref=plane_row, dst_ref=stats_out.at[slot],
            send_sem=b_send.at[rel], recv_sem=b_recv.at[slot],
            device_id=(grp, 2 * plane_at(rel) + core), device_id_type=MESH)

    def stat_out_arrive(rel):
        return pltpu.make_async_remote_copy(
            src_ref=plane_row, dst_ref=stats_out.at[rel],
            send_sem=b_send.at[rel], recv_sem=b_recv.at[rel],
            device_id=(grp, 2 * plane_at(rel) + core), device_id_type=MESH)

    stat_row[...] = jnp.sum(stat_acc[...], axis=0, keepdims=True)

    def send_stat(d, c):
        stat_in_copy(d).start()
        return c

    over_plane(send_stat)

    def arrive(u):
        pltpu.make_async_copy(recv.at[u], recv.at[u], f_recv.at[u]).wait()

    def product(u, v):
        total = None
        for r in range(ranks):
            term = lax.dot_general(
                recv[u, r], recv[v, r], NT, preferred_element_type=jnp.float32)
            total = term if total is None else total + term
        return total

    ones = jnp.ones((8, span), jnp.bfloat16)
    scale = 1.0 / math.sqrt(width)

    def sums(u):
        total = None
        for r in range(ranks):
            term = lax.dot_general(ones, recv[u, r], NT, preferred_element_type=jnp.float32)
            total = term if total is None else total + term
        prow_part[:, u * unit:(u + 1) * unit] = total[:1] * scale

    partner = (grp, blk + 1 - 2 * core)
    across = (grp + 1 - 2 * side, blk)

    def spot(i):
        (i0, j0), (i1, j1) = TILES[2 * i], TILES[2 * i + 1]
        return i0 + core * (i1 - i0), j0 + core * (j1 - j0)

    def spot_ref(i):
        at, to = spot(i)
        return full.at[pl.ds(pl.multiple_of(at * unit, unit), unit),
                       pl.ds(pl.multiple_of(to * unit, unit), unit)]

    def give(i):
        return pltpu.make_async_remote_copy(
            src_ref=part.at[2 * i + 1 - core], dst_ref=land1.at[i],
            send_sem=s_send.at[3 * i], recv_sem=s_recv.at[3 * i],
            device_id=partner, device_id_type=MESH)

    def swap(i):
        return pltpu.make_async_remote_copy(
            src_ref=part.at[2 * i + core], dst_ref=land2.at[i],
            send_sem=s_send.at[3 * i + 1], recv_sem=s_recv.at[3 * i + 1],
            device_id=across, device_id_type=MESH)

    def share(i):
        return pltpu.make_async_remote_copy(
            src_ref=spot_ref(i), dst_ref=spot_ref(i),
            send_sem=s_send.at[3 * i + 2], recv_sem=s_recv.at[3 * i + 2],
            device_id=partner, device_id_type=MESH)

    def second(i):
        give(i).wait_recv()
        mine = 2 * i + core
        part[mine] = part[mine] + land1[i]
        swap(i).start()

    def third(i):
        swap(i).wait_recv()
        at, to = spot(i)
        full[pl.ds(pl.multiple_of(at * unit, unit), unit),
             pl.ds(pl.multiple_of(to * unit, unit), unit)] = part[2 * i + core] + land2[i]
        share(i).start()

    def mirror(t):
        at, to = TILES[t]
        if at != to:
            a, b = slice(at * unit, (at + 1) * unit), slice(to * unit, (to + 1) * unit)
            full[b, a] = full[a, b].T

    def prow_copy(m):
        pg = grp + (1 - 2 * side) * (m % 2)
        pb = blk + (1 - 2 * core) * (m // 2)
        return pltpu.make_async_remote_copy(
            src_ref=prow_part, dst_ref=prow_land.at[m - 1],
            send_sem=p_send.at[m - 1], recv_sem=p_recv.at[m - 1],
            device_id=(pg, pb), device_id_type=MESH)

    last = UNITS - 1
    pairs = len(TILES) // 2
    early = [i for i in range(pairs) if TILES[2 * i + 1][0] < last]
    late = [i for i in range(pairs) if TILES[2 * i][0] == last]
    sent = 0
    for u in range(last):
        arrive(u)
        sums(u)
        for v in range(u + 1):
            part[u * (u + 1) // 2 + v] = product(u, v)
        if u == 0:
            def arrive_stat(d, c):
                stat_in_copy(d).wait_recv()
                return c

            over_plane(arrive_stat)
            stats_in[0] = stat_row[...]
            plane_row[...] = jnp.sum(stats_in[...], axis=0)
            for rel in range(1, planes):
                stat_out_copy(rel).start()
            stats_out[0] = plane_row[...]
        while sent < len(early) and 2 * sent + 1 < (u + 1) * (u + 2) // 2:
            give(sent).start()
            sent += 1
        if u == last - 1:
            for i in early:
                second(i)
            for i in early:
                third(i)
    arrive(last)
    base = last * (last + 1) // 2
    for n, i in enumerate(late):
        v = 2 * n + 1 - core
        part[base + v] = product(last, v)
        give(i).start()
    sums(last)
    for m in range(1, 4):
        prow_copy(m).start()
    for n, i in enumerate(late):
        v = 2 * n + core
        part[base + v] = product(last, v)
        second(i)
    for i in early:
        share(i).wait_recv()
    for t in range(base):
        mirror(t)
    for rel in range(1, planes):
        stat_out_arrive(rel).wait_recv()
    total = jnp.sum(jnp.sum(stats_out[...], axis=0), axis=1, keepdims=True)
    damping = damping_rate * total / (width * blocks)

    def rel_row(q, pc, ch):
        rel = seen_from(q, plane)
        u = 2 * lax.div(rel, near) + ch
        return u * unit + ((lax.rem(rel, near) * groups + solved) * 2 + pc) * ex_c

    pieces = [(q, pc, ch) for q in range(planes) for pc in range(2) for ch in range(CHUNKS)]
    lane = lax.broadcasted_iota(jnp.int32, (2 * ex_c, total_ex), 1)
    sub = lax.broadcasted_iota(jnp.int32, (2 * ex_c, total_ex), 0)
    for n in range(0, len(pieces), 2):
        a, b = rel_row(*pieces[n]), rel_row(*pieces[n + 1])
        at = jnp.where(sub < ex_c, a + sub, b + sub - ex_c)
        pick[n * ex_c:(n + 2) * ex_c, :] = jnp.where(at == lane, 1.0, 0.0).astype(jnp.bfloat16)

    for m in range(1, 4):
        prow_copy(m).wait_recv()
    row[...] = jnp.broadcast_to(prow_part[...] + jnp.sum(prow_land[...], axis=0), row.shape)
    for i in late:
        third(i)
    for i in late:
        share(i).wait_recv()
    for t in range(base, len(TILES)):
        mirror(t)

    tile = 128
    tiles = total_ex // tile

    def tile_rows(i):
        return pl.ds(pl.multiple_of(i * tile, tile), tile)

    def turn(i, c):
        spots = lax.broadcasted_iota(jnp.int32, (tile, total_ex), 0) + i * tile
        lanes = lax.broadcasted_iota(jnp.int32, (tile, total_ex), 1)
        picked = jnp.where(spots == lanes, row[:1, :], 0.0)
        col[tile_rows(i), :] = jnp.broadcast_to(
            jnp.sum(picked, axis=1, keepdims=True), (tile, 128))
        return c

    lax.fori_loop(0, tiles, turn, 0)
    top = None
    for step in range(power_steps):
        final = step + 1 == power_steps
        prow = row[:1, :]

        def image(i, acc):
            k_tile = full[tile_rows(i), :]
            if not final:
                col_next[tile_rows(i), :] = jnp.broadcast_to(
                    jnp.sum(k_tile * prow, axis=1, keepdims=True), (tile, 128))
            return acc + jnp.sum(k_tile * col[tile_rows(i), :][:, :1], axis=0, keepdims=True)

        q = lax.fori_loop(0, tiles, image, jnp.zeros((1, total_ex), jnp.float32))
        square = jnp.sum(prow * q, axis=1, keepdims=True)
        top = jnp.sqrt(jnp.maximum(square, 0.0) + 1e-06)
        if not final:
            row[...] = jnp.broadcast_to(q / top, row.shape)
            col[...] = col_next[...] / top

    center = damping + top
    rho, delta = top / center, damping / center
    zero, one = jnp.zeros_like(center), jnp.ones_like(center)

    def shifted(p):
        low = [delta * v for v in p] + [zero]
        return [a + b for a, b in zip(low, [zero] + list(p))]

    def plus(p, q, factor):
        n = max(len(p), len(q))
        p = list(p) + [zero] * (n - len(p))
        q = list(q) + [zero] * (n - len(q))
        return [a + factor * b for a, b in zip(p, q)]

    sig = one
    direction = [one]
    solution_poly = [one]
    residual = plus([one], shifted(direction), -sig)
    for sweep in range(1, ITERS):
        momentum = 0.5 * (rho * sig) ** 2 if sweep == 1 else (0.5 * rho * sig) ** 2
        sig = 1.0 / (1.0 - momentum / sig)
        direction = plus(residual, direction, momentum)
        solution_poly = plus(solution_poly, direction, sig)
        if sweep + 1 < ITERS:
            residual = plus(residual, shifted(direction), -sig)
    s0, s1, s2, s3 = solution_poly

    inverse = 1.0 / center
    for n, piece in enumerate(pieces):
        y_ref[n * ex_c:(n + 1) * ex_c, :] = (
            full[pl.ds(pl.multiple_of(rel_row(*piece), ex_c), ex_c), :] * inverse)
    step_ex = min(256, total_ex)

    def halves(v):
        high = v.astype(jnp.bfloat16)
        return high, (v - high.astype(jnp.float32)).astype(jnp.bfloat16)

    def nt(x, y):
        return lax.dot_general(x, y, NT, preferred_element_type=jnp.float32)

    def dot_nt(a, b):
        (a_high, a_low), (b_high, b_low) = halves(a), halves(b)
        return nt(a_high, b_high) + (nt(a_high, b_low) + nt(a_low, b_high))

    sc[...] = jnp.zeros_like(sc)

    def solve(j, c):
        at = pl.ds(pl.multiple_of(j * step_ex, step_ex), step_ex)
        y_tile = y_ref[:, at]
        z_tile = dot_nt(y_ref[...], full[at, :] * inverse)
        y_high, y_low = halves(y_tile)
        sc[...] += (s0 * (nt(y_high, pick[:, at]) + nt(y_low, pick[:, at]))
                    + dot_nt(y_tile, s1 * y_tile + s2 * z_tile) + dot_nt(z_tile, s3 * z_tile))
        return c

    lax.fori_loop(0, total_ex // step_ex, solve, 0)

    block = 2 * plane + row_of

    def score_copy(b):
        start = pl.multiple_of(b * examples, examples)
        return pltpu.make_async_remote_copy(
            src_ref=sc.at[pl.ds(start, examples)], dst_ref=sc_land.at[block],
            send_sem=o_send.at[b], recv_sem=o_recv.at[block],
            device_id=(solved, b), device_id_type=MESH)

    def score_self():
        start = pl.multiple_of(blk * examples, examples)
        return pltpu.make_async_copy(
            sc.at[pl.ds(start, examples)], sc_land.at[block], o_recv.at[block])

    def score_send(d, c):
        score_copy(lax.rem(blk + d, blocks)).start()
        return c

    lax.fori_loop(1, blocks, score_send, 0)

    @pl.when(solved == grp)
    def _():
        score_self().start()

    @pl.when(solved != grp)
    def _():
        score_copy(blk).start()

    def score_arrive(k, c):
        pltpu.make_async_copy(sc_land.at[k], sc_land.at[k], o_recv.at[k]).wait()
        return c

    lax.fori_loop(0, blocks, score_arrive, 0)
    out_ref[...] = jnp.sum(sc_land[...], axis=0)

    for chunk in range(CHUNKS):
        whole = feat.at[chunk, pl.ds(0, devices - 1)]
        pltpu.make_async_copy(whole, whole, f_send.at[chunk]).wait()

    def stat_gone(d, c):
        stat_in_copy(d).wait_send()
        return c

    over_plane(stat_gone)
    for rel in range(1, planes):
        stat_out_copy(rel).wait_send()
    for i in range(pairs):
        give(i).wait_send()
        swap(i).wait_send()
        share(i).wait_send()
    for m in range(1, 4):
        prow_copy(m).wait_send()

    def score_gone(d, c):
        score_copy(lax.rem(blk + d, blocks)).wait_send()
        return c

    lax.fori_loop(1, blocks, score_gone, 0)

    @pl.when(solved != grp)
    def _():
        score_copy(blk).wait_send()


def shards(groups, blocks, activations, out_grads, proj_act, proj_out):
    tokens, depth = activations.shape
    examples = tokens // SEQ
    rank, span = proj_act.shape[1], proj_out.shape[1]
    devices = groups * blocks
    group_ex, total_ex = examples * blocks, examples * devices
    ranks = rank // devices
    width = rank * span // blocks
    planes, unit = blocks // 2, total_ex // UNITS
    ex_c, rows_l = examples // CHUNKS, tokens // PARTS
    slots = PARTS if total_ex <= 1024 else PARTS // 2
    vmem = pl.BlockSpec(memory_space=pltpu.VMEM)
    hbm = pl.BlockSpec(memory_space=pl.ANY)
    f32, low = jnp.float32, jnp.bfloat16
    dma = pltpu.SemaphoreType.DMA
    tiles = len(TILES)
    scores = pl.pallas_call(
        functools.partial(mix_kernel, groups, blocks, examples, ranks, width, slots),
        out_shape=jax.ShapeDtypeStruct((examples, group_ex), f32),
        in_specs=[hbm] * 4,
        out_specs=vmem,
        scratch_shapes=[
            pltpu.VMEM((slots, rows_l, depth), low),
            pltpu.VMEM((slots, rows_l, depth), low),
            pltpu.VMEM((depth, rank), low),
            pltpu.VMEM((depth, span), low),
            pltpu.VMEM((span // 128, rank * ex_c, 128), f32),
            pltpu.VMEM((CHUNKS, devices, ranks, ex_c, span), low),
            pltpu.VMEM((UNITS, ranks, unit, span), low),
            pltpu.VMEM((8, 128), f32),
            pltpu.VMEM((1, 128), f32),
            pltpu.VMEM((2 * groups, 1, 128), f32),
            pltpu.VMEM((1, 128), f32),
            pltpu.VMEM((planes, 1, 128), f32),
            pltpu.VMEM((tiles, unit, unit), f32),
            pltpu.VMEM((tiles // 2, unit, unit), f32),
            pltpu.VMEM((tiles // 2, unit, unit), f32),
            pltpu.VMEM((total_ex, total_ex), f32),
            pltpu.VMEM((1, total_ex), f32),
            pltpu.VMEM((3, 1, total_ex), f32),
            pltpu.VMEM((8, total_ex), f32),
            pltpu.VMEM((total_ex, 128), f32),
            pltpu.VMEM((total_ex, 128), f32),
            pltpu.VMEM((group_ex, total_ex), f32),
            pltpu.VMEM((group_ex, total_ex), low),
            pltpu.VMEM((group_ex, group_ex), f32),
            pltpu.VMEM((blocks, examples, group_ex), f32),
            dma((2 * slots,)), dma((2,)), dma((CHUNKS,)), dma((UNITS,)),
            dma((2 * groups,)), dma((2 * groups,)), dma((planes,)), dma((planes,)),
            dma((3 * tiles // 2,)), dma((3 * tiles // 2,)), dma((3,)), dma((3,)),
            dma((blocks,)), dma((blocks,)),
        ],
        compiler_params=pltpu.CompilerParams(
            collective_id=0, has_side_effects=True, vmem_limit_bytes=67043328
        ),
    )(activations, out_grads, proj_act, proj_out)
    return scores * float(examples * groups)


def solution(mesh):
    in_specs = (P(("grp", "blk"), None), P(("grp", "blk"), None), P(), P())
    out_specs = P(("grp", "blk"), None)
    body = functools.partial(shards, mesh.shape["grp"], mesh.shape["blk"])
    return jax.shard_map(body, mesh=mesh, in_specs=in_specs, out_specs=out_specs, check_vma=False)
```

```python
import functools
import math

import jax
import jax.numpy as jnp
from jax import lax
from jax.experimental import pallas as pl
from jax.experimental.pallas import tpu as pltpu
from jax.sharding import PartitionSpec as P

SEQ = 64
ITERS = 4
damping_rate = 0.5
power_steps = 3
CHUNKS = 2
PARTS = 4
AHEAD = 2
UNITS = 4
MESH = pl.DeviceIdType.MESH
NT = (((1,), (1,)), ((), ()))
TN = (((0,), (0,)), ((), ()))
TILES = [(i, j) for i in range(UNITS) for j in range(i + 1)]


def mix_kernel(
    groups, blocks, examples, ranks, width, slots, batch, keep,
    act_hbm, grad_hbm, pact_hbm, pout_hbm, out_ref,
    act_buf, grad_buf, pact, pout, wide, feat, recv, stat_acc, stat_row, stats,
    land, full, w_high, w_low, prow_part, prow_land, row, col, y_high, y_low, pick, acc, sc, sc_land,
    l_sem, w_sem, f_send, f_recv, t_send, t_recv, k_send, k_recv, p_send, p_recv, o_send, o_recv,
):
    devices = groups * blocks
    planes = blocks // 2
    near = planes // 2
    targets = 2 * blocks
    group_ex = examples * blocks
    total_ex = group_ex * groups
    unit = total_ex // UNITS
    span = recv.shape[3]
    ex_c = examples // CHUNKS
    core_groups = groups // 2
    grp, blk = lax.axis_index("grp"), lax.axis_index("blk")
    me = grp * blocks + blk
    core, plane = lax.rem(blk, 2), lax.div(blk, 2)
    sign = 1 - 2 * lax.rem(plane, 2)
    far_end = groups - 1
    is_owner = lax.rem(grp, far_end) == 0
    block = 2 * plane + lax.div(grp, far_end)

    def plane_at(rel):
        return lax.rem(plane + sign * rel + planes, planes)

    def seen_from(source, target):
        flip = 1 - 2 * lax.rem(target, 2)
        return lax.rem((source - target) * flip + planes, planes)

    def target_of(d):
        rel = lax.rem(near + lax.div(d, 4), planes)
        j = lax.rem(d, 4)
        side = lax.rem(grp + lax.div(j, 2), 2)
        pc = lax.rem(core + lax.rem(j, 2), 2)
        return side, plane_at(rel), pc

    barrier = pltpu.get_barrier_semaphore()

    def greet(d, c):
        peer = lax.rem(me + d, devices)
        pl.semaphore_signal(
            barrier, inc=1, device_id=(lax.div(peer, blocks), lax.rem(peer, blocks)),
            device_id_type=MESH)
        return c

    rows_l = act_buf.shape[1]

    def load(k):
        at = pl.ds(k * rows_l, rows_l)
        return (
            pltpu.make_async_copy(act_hbm.at[at], act_buf.at[k % slots], l_sem.at[2 * (k % slots)]),
            pltpu.make_async_copy(grad_hbm.at[at], grad_buf.at[k % slots], l_sem.at[2 * (k % slots) + 1]),
        )

    load_pact = pltpu.make_async_copy(pact_hbm, pact, w_sem.at[0])
    load_pout = pltpu.make_async_copy(pout_hbm, pout, w_sem.at[1])
    load_pact.start()
    load_pout.start()
    for k in range(AHEAD):
        for c in load(k):
            c.start()
    lax.fori_loop(1, devices, greet, 0)
    stat_acc[...] = jnp.zeros_like(stat_acc)

    per_part = rows_l // SEQ
    parts_c = PARTS // CHUNKS

    def project(k):
        loads = load(k)
        if k == 0:
            load_pact.wait()
            load_pout.wait()
        for c in loads:
            c.wait()
        if k + AHEAD < PARTS and AHEAD < slots:
            for c in load(k + AHEAD):
                c.start()
        a_low = jnp.dot(
            act_buf[k % slots], pact[...], preferred_element_type=jnp.float32
        ).astype(jnp.bfloat16)
        g_low = jnp.dot(
            grad_buf[k % slots], pout[...], preferred_element_type=jnp.float32
        ).astype(jnp.bfloat16)
        if k + AHEAD < PARTS and AHEAD == slots:
            for c in load(k + AHEAD):
                c.start()
        for e in range(per_part):
            here = slice(e * SEQ, (e + 1) * SEQ)
            product = lax.dot_general(
                a_low[here], g_low[here], TN, preferred_element_type=jnp.float32)
            at = (k % parts_c) * per_part + e
            for h in range(wide.shape[0]):
                wide[h, pl.ds(at, a_low.shape[1], stride=ex_c), :] = (
                    product[:, h * 128:(h + 1) * 128])

    def narrow(chunk, slot):
        for r in range(ranks):
            rows = pl.ds(pl.multiple_of((slot * ranks + r) * ex_c, ex_c), ex_c)
            for h in range(wide.shape[0]):
                low = wide[h, rows, :].astype(jnp.bfloat16)
                feat[chunk, slot, r, :, h * 128:(h + 1) * 128] = low
                back = low.astype(jnp.float32)
                stat_acc[...] += jnp.sum((back * back).reshape(ex_c // 8, 8, 128), axis=0)

    def landing(chunk, pp):
        rel = seen_from(plane, pp)
        u = 2 * lax.div(rel, near) + chunk
        at = (lax.rem(rel, near) * groups + grp) * 2 + core
        return recv.at[u, :, pl.ds(pl.multiple_of(at * ex_c, ex_c), ex_c), :], u

    def either(side, pp, pc, local, remote):
        mine = jnp.logical_and(side * far_end == grp, 2 * pp + pc == blk)
        pl.when(mine)(local)
        pl.when(jnp.logical_not(mine))(remote)

    for chunk in range(CHUNKS):
        for k in range(parts_c):
            project(chunk * parts_c + k)
        if chunk == 0:
            pl.semaphore_wait(barrier, devices - 1)

        def send(d, c, chunk=chunk):
            side, pp, pc = target_of(d)
            slot = (2 * pp + side) * 2 + pc
            narrow(chunk, slot)
            dst, u = landing(chunk, pp)

            def local():
                pltpu.make_async_copy(feat.at[chunk, slot], dst, f_recv.at[u]).start()

            def remote():
                pltpu.make_async_remote_copy(
                    src_ref=feat.at[chunk, slot], dst_ref=dst,
                    send_sem=f_send.at[chunk], recv_sem=f_recv.at[u],
                    device_id=(side * far_end, 2 * pp + pc), device_id_type=MESH).start()

            either(side, pp, pc, local, remote)
            return c

        lax.fori_loop(0, targets, send, 0)

    stat_row[...] = jnp.sum(stat_acc[...], axis=0, keepdims=True)

    def send_stat(d, c):
        side, pp, pc = target_of(d)

        def local():
            pltpu.make_async_copy(stat_row, stats.at[me], t_recv).start()

        def remote():
            pltpu.make_async_remote_copy(
                src_ref=stat_row, dst_ref=stats.at[me], send_sem=t_send, recv_sem=t_recv,
                device_id=(side * far_end, 2 * pp + pc), device_id_type=MESH).start()

        either(side, pp, pc, local, remote)
        return c

    lax.fori_loop(0, targets, send_stat, 0)

    ones = jnp.ones((8, span), jnp.bfloat16)
    norm = 1.0 / math.sqrt(width)
    partner = (grp, blk + 1 - 2 * core)
    pieces = [(q, pc, ch) for q in range(planes) for pc in range(2) for ch in range(CHUNKS)]

    def nt(x, y):
        return lax.dot_general(x, y, NT, preferred_element_type=jnp.float32)

    def halves(v):
        high = v.astype(jnp.bfloat16)
        return high, (v - high.astype(jnp.float32)).astype(jnp.bfloat16)

    def arrive(u):
        pltpu.make_async_copy(recv.at[u], recv.at[u], f_recv.at[u]).wait()

    def over_ranks(left, v):
        total = None
        for r in range(ranks):
            term = nt(left(r), recv[v, r])
            total = term if total is None else total + term
        return total

    def area(u, v):
        return slice(u * unit, (u + 1) * unit), slice(v * unit, (v + 1) * unit)

    def tile_copy(u, v):
        t = u * (u + 1) // 2 + v
        a, b = area(u, v)
        return pltpu.make_async_remote_copy(
            src_ref=full.at[a, b], dst_ref=land.at[t],
            send_sem=k_send.at[t], recv_sem=k_recv.at[t],
            device_id=partner, device_id_type=MESH)

    def prow_copy():
        return pltpu.make_async_remote_copy(
            src_ref=prow_part, dst_ref=prow_land, send_sem=p_send, recv_sem=p_recv,
            device_id=partner, device_id_type=MESH)

    def rel_row(group, q, pc, ch):
        rel = seen_from(q, plane)
        u = 2 * lax.div(rel, near) + ch
        return u * unit + ((lax.rem(rel, near) * groups + group) * 2 + pc) * ex_c

    def own_work():
        for u in range(UNITS):
            arrive(u)
            if u == 0:
                pltpu.make_async_copy(stats, stats, t_recv).wait()
            total = jnp.sum(jnp.sum(stats[...], axis=0), axis=1, keepdims=True)
            shrink = 1.0 / (total + 1e-30)
            for v in range(u + 1):
                a, b = area(u, v)
                full[a, b] = over_ranks(lambda r, u=u: recv[u, r], v)
                tile_copy(u, v).start()
            prow_part[:, u * unit:(u + 1) * unit] = over_ranks(lambda r: ones, u)[:1] * norm
            if u == UNITS - 1:
                prow_copy().start()
            for v in range(u + 1):
                t = u * (u + 1) // 2 + v
                a, b = area(u, v)
                tile_copy(u, v).wait_recv()
                tile_copy(u, v).wait_send()
                both = full[a, b] + land[t]
                full[a, b] = both
                if keep:
                    w_high[a, b], w_low[a, b] = halves(both * shrink)
                if u != v:
                    both = both.T
                    full[b, a] = both
                    if keep:
                        w_high[b, a], w_low[b, a] = halves(both * shrink)
        damping = damping_rate * total / (width * blocks)
        prow_copy().wait_recv()
        prow_copy().wait_send()

        row[...] = jnp.broadcast_to(prow_part[...] + prow_land[...], row.shape)

        def upright(values):
            for c in range(total_ex // 128):
                here = slice(c * 128, (c + 1) * 128)
                col[here, :] = jnp.broadcast_to(values[:, here], (128, 128)).T

        def image():
            def block_sum(i, total):
                for e in range(16):
                    rows = pl.ds(i * 128 + e * 8, 8)
                    weight = jnp.concatenate([col[rows, :]] * (total_ex // 128), axis=1)
                    total = total + full[rows, :] * weight
                return total

            start = jnp.zeros((8, total_ex), jnp.float32)
            if total_ex <= 512:
                for i in range(total_ex // 128):
                    start = block_sum(i, start)
            else:
                start = lax.fori_loop(
                    0, total_ex // 128,
                    lambda i, t: block_sum(i, t), start)
            return jnp.sum(start, axis=0, keepdims=True)

        step_ex = min(256, total_ex)

        def prepare(first):
            for n in range(batch):
                group = core * core_groups + first + n
                for m in range(0, len(pieces), 2):
                    at, to = rel_row(group, *pieces[m]), rel_row(group, *pieces[m + 1])
                    at, to = pl.multiple_of(at, ex_c), pl.multiple_of(to, ex_c)
                    y = jnp.concatenate(
                        [full[pl.ds(at, ex_c), :], full[pl.ds(to, ex_c), :]], axis=0) * shrink
                    here = slice(n * group_ex + m * ex_c, n * group_ex + (m + 2) * ex_c)
                    y_high[here, :], y_low[here, :] = halves(y)
                    lane = lax.broadcasted_iota(jnp.int32, (2 * ex_c, total_ex), 1)
                    sub = lax.broadcasted_iota(jnp.int32, (2 * ex_c, total_ex), 0)
                    spot = jnp.where(sub < ex_c, at + sub, to + sub - ex_c)
                    pick[here, :] = jnp.where(spot == lane, 1.0, 0.0).astype(jnp.bfloat16)

        def powers(at, fresh):
            yh, yl = y_high[...], y_low[...]
            if keep:
                wh, wl = w_high[at, :], w_low[at, :]
            else:
                wh, wl = halves(full[at, :] * shrink)
            vh, vl = halves(nt(yh, wh) + (nt(yh, wl) + nt(yl, wh)))
            for n in range(batch):
                here = slice(n * group_ex, (n + 1) * group_ex)
                ah, al, ph = y_high[here, at], y_low[here, at], pick[here, at]
                bh, bl = vh[here], vl[here]
                right = jnp.concatenate([ah, ph], axis=0)
                one = nt(ah, right) + nt(al, right)
                one_low = nt(ah, al)
                both_h = jnp.concatenate([ah, bh], axis=0)
                both_l = jnp.concatenate([al, bl], axis=0)
                two = nt(bh, both_h) + (nt(bh, both_l) + nt(bl, both_h))
                terms = (one[:, group_ex:], one[:, :group_ex] + one_low,
                         two[:, :group_ex], two[:, group_ex:])
                for k, term in enumerate(terms):
                    acc[n, k] = term if fresh else acc[n, k] + term

        def multiply():
            if total_ex <= 512:
                for k in range(total_ex // step_ex):
                    powers(slice(k * step_ex, (k + 1) * step_ex), k == 0)
            else:
                acc[...] = jnp.zeros_like(acc)

                def one_step(k, c):
                    powers(pl.ds(pl.multiple_of(k * step_ex, step_ex), step_ex), False)
                    return c

                lax.fori_loop(0, total_ex // step_ex, one_step, 0)

        prepare(0)
        multiply()
        values = row[:1, :]
        top = None
        for step in range(power_steps):
            upright(values)
            q = image()
            square = jnp.sum(values * q, axis=1, keepdims=True)
            top = jnp.sqrt(jnp.maximum(square, 0.0) + 1e-06)
            values = q / top

        center = damping + top
        rho, delta = top / center, damping / center
        zero, one = jnp.zeros_like(center), jnp.ones_like(center)

        def shifted(p):
            low = [delta * v for v in p] + [zero]
            return [a + b for a, b in zip(low, [zero] + list(p))]

        def plus(p, q, factor):
            n = max(len(p), len(q))
            p = list(p) + [zero] * (n - len(p))
            q = list(q) + [zero] * (n - len(q))
            return [a + factor * b for a, b in zip(p, q)]

        sig = one
        direction = [one]
        solution_poly = [one]
        residual = plus([one], shifted(direction), -sig)
        for sweep in range(1, ITERS):
            momentum = 0.5 * (rho * sig) ** 2 if sweep == 1 else (0.5 * rho * sig) ** 2
            sig = 1.0 / (1.0 - momentum / sig)
            direction = plus(residual, direction, momentum)
            solution_poly = plus(solution_poly, direction, sig)
            if sweep + 1 < ITERS:
                residual = plus(residual, shifted(direction), -sig)
        stretch = (total + 1e-30) / center
        factors = []
        power = stretch
        for coefficient in solution_poly:
            factors.append(coefficient * power)
            power = power * stretch

        for first in range(0, core_groups, batch):
            if first:
                prepare(first)
                multiply()
            for n in range(batch):
                score = factors[0] * acc[n, 0]
                for k in range(1, ITERS):
                    score = score + factors[k] * acc[n, k]
                sc[first + n] = score

                def send_score(d, c, n=first + n):
                    b = lax.rem(blk + blocks // 2 + d, blocks)
                    group = core * core_groups + n
                    src = sc.at[n, pl.ds(pl.multiple_of(b * examples, examples), examples)]
                    mine = jnp.logical_and(group == grp, b == blk)

                    @pl.when(mine)
                    def _():
                        pltpu.make_async_copy(src, sc_land.at[block], o_recv.at[block]).start()

                    @pl.when(jnp.logical_not(mine))
                    def _():
                        pltpu.make_async_remote_copy(
                            src_ref=src, dst_ref=sc_land.at[block],
                            send_sem=o_send.at[n * blocks + b], recv_sem=o_recv.at[block],
                            device_id=(group, b), device_id_type=MESH).start()

                    return c

                lax.fori_loop(0, blocks, send_score, 0)

    pl.when(is_owner)(own_work)

    def score_arrive(k, c):
        pltpu.make_async_copy(sc_land.at[k], sc_land.at[k], o_recv.at[k]).wait()
        return c

    lax.fori_loop(0, blocks, score_arrive, 0)
    out_ref[...] = jnp.sum(sc_land[...], axis=0)

    def gone(count):
        for chunk in range(CHUNKS):
            sent = feat.at[chunk, pl.ds(0, count)]
            pltpu.make_async_copy(sent, sent, f_send.at[chunk]).wait()
        rows = stats.at[pl.ds(0, count)]
        pltpu.make_async_copy(rows, rows, t_send).wait()

    @pl.when(is_owner)
    def _():
        gone(targets - 1)
        for n in range(core_groups):
            def score_gone(d, c, n=n):
                b = lax.rem(blk + d, blocks)
                group = core * core_groups + n
                src = sc.at[n, pl.ds(pl.multiple_of(b * examples, examples), examples)]

                @pl.when(jnp.logical_not(jnp.logical_and(group == grp, b == blk)))
                def _():
                    pltpu.make_async_copy(src, src, o_send.at[n * blocks + b]).wait()

                return c

            lax.fori_loop(0, blocks, score_gone, 0)

    @pl.when(jnp.logical_not(is_owner))
    def _():
        gone(targets)


def shards(groups, blocks, activations, out_grads, proj_act, proj_out):
    tokens, depth = activations.shape
    examples = tokens // SEQ
    rank, span = proj_act.shape[1], proj_out.shape[1]
    devices, targets = groups * blocks, 2 * blocks
    group_ex, total_ex = examples * blocks, examples * devices
    ranks = rank // targets
    width = rank * span // blocks
    unit = total_ex // UNITS
    ex_c, rows_l = examples // CHUNKS, tokens // PARTS
    small = total_ex <= 1024
    slots = PARTS if small else AHEAD
    batch = groups // 2 if small else 1
    split = total_ex if small else 8
    vmem = pl.BlockSpec(memory_space=pltpu.VMEM)
    hbm = pl.BlockSpec(memory_space=pl.ANY)
    f32, low = jnp.float32, jnp.bfloat16
    dma = pltpu.SemaphoreType.DMA
    tiles = len(TILES)
    scores = pl.pallas_call(
        functools.partial(mix_kernel, groups, blocks, examples, ranks, width, slots, batch, small),
        out_shape=jax.ShapeDtypeStruct((examples, group_ex), f32),
        in_specs=[hbm] * 4,
        out_specs=vmem,
        scratch_shapes=[
            pltpu.VMEM((slots, rows_l, depth), low),
            pltpu.VMEM((slots, rows_l, depth), low),
            pltpu.VMEM((depth, rank), low),
            pltpu.VMEM((depth, span), low),
            pltpu.VMEM((span // 128, rank * ex_c, 128), f32),
            pltpu.VMEM((CHUNKS, targets, ranks, ex_c, span), low),
            pltpu.VMEM((UNITS, ranks, unit, span), low),
            pltpu.VMEM((8, 128), f32),
            pltpu.VMEM((1, 128), f32),
            pltpu.VMEM((devices, 1, 128), f32),
            pltpu.VMEM((tiles, unit, unit), f32),
            pltpu.VMEM((total_ex, total_ex), f32),
            pltpu.VMEM((split, total_ex), low),
            pltpu.VMEM((split, total_ex), low),
            pltpu.VMEM((1, total_ex), f32),
            pltpu.VMEM((1, total_ex), f32),
            pltpu.VMEM((8, total_ex), f32),
            pltpu.VMEM((total_ex, 128), f32),
            pltpu.VMEM((batch * group_ex, total_ex), low),
            pltpu.VMEM((batch * group_ex, total_ex), low),
            pltpu.VMEM((batch * group_ex, total_ex), low),
            pltpu.VMEM((batch, ITERS, group_ex, group_ex), f32),
            pltpu.VMEM((groups // 2, group_ex, group_ex), f32),
            pltpu.VMEM((blocks, examples, group_ex), f32),
            dma((2 * slots,)), dma((2,)), dma((CHUNKS,)), dma((UNITS,)), dma, dma,
            dma((tiles,)), dma((tiles,)), dma, dma,
            dma((groups // 2 * blocks,)), dma((blocks,)),
        ],
        compiler_params=pltpu.CompilerParams(
            collective_id=0, has_side_effects=True, vmem_limit_bytes=67043328
        ),
    )(activations, out_grads, proj_act, proj_out)
    return scores * float(examples * groups)


def solution(mesh):
    in_specs = (P(("grp", "blk"), None), P(("grp", "blk"), None), P(), P())
    out_specs = P(("grp", "blk"), None)
    body = functools.partial(shards, mesh.shape["grp"], mesh.shape["blk"])
    return jax.shard_map(body, mesh=mesh, in_specs=in_specs, out_specs=out_specs, check_vma=False)
```

```python
import functools
import math

import jax
import jax.numpy as jnp
from jax import lax
from jax.experimental import pallas as pl
from jax.experimental.pallas import tpu as pltpu
from jax.sharding import PartitionSpec as P

SEQ = 64
ITERS = 4
damping_rate = 0.5
power_steps = 3
CHUNKS = 2
PARTS = 4
AHEAD = 2
MESH = pl.DeviceIdType.MESH
NT = (((1,), (1,)), ((), ()))
TN = (((0,), (0,)), ((), ()))
TILES = [(i, j) for i in range(CHUNKS) for j in range(i + 1)]


def mix_kernel(
    groups, blocks, examples, ranks, width, slots, batch, keep,
    act_hbm, grad_hbm, pact_hbm, pout_hbm, out_ref,
    act_buf, grad_buf, pact, pout, wide, feat, recv, stat_acc, stat_row, stats,
    land, full, w_high, w_low, prow_part, prow_land, row, col, y_high, y_low, pick, acc, sc, sc_land,
    l_sem, w_sem, f_send, f_recv, t_send, t_recv, k_send, k_recv, p_send, p_recv, o_send, o_recv,
):
    devices = groups * blocks
    planes = blocks // 2
    far = planes // 2
    targets = 2 * blocks
    group_ex = examples * blocks
    total_ex = group_ex * groups
    unit = total_ex // CHUNKS
    span = recv.shape[2]
    ex_c = examples // CHUNKS
    core_groups = groups // 2
    grp, blk = lax.axis_index("grp"), lax.axis_index("blk")
    me = grp * blocks + blk
    core, plane = lax.rem(blk, 2), lax.div(blk, 2)
    sign = 1 - 2 * lax.rem(plane, 2)
    far_end = groups - 1
    is_owner = lax.rem(grp, far_end) == 0
    block = 2 * plane + lax.div(grp, far_end)

    def plane_at(rel):
        return lax.rem(plane + sign * rel + planes, planes)

    def seen_from(source, target):
        flip = 1 - 2 * lax.rem(target, 2)
        return lax.rem((source - target) * flip + planes, planes)

    def target_of(d):
        n = lax.div(d, 4)
        rel = lax.rem(far - n + planes, planes)
        j = lax.rem(d, 4)
        side = lax.rem(grp + lax.div(j, 2), 2)
        pc = lax.rem(core + lax.rem(j, 2), 2)
        return side, plane_at(rel), pc

    barrier = pltpu.get_barrier_semaphore()

    def greet(d, c):
        peer = lax.rem(me + d, devices)
        pl.semaphore_signal(
            barrier, inc=1, device_id=(lax.div(peer, blocks), lax.rem(peer, blocks)),
            device_id_type=MESH)
        return c

    rows_l = act_buf.shape[1]

    def load(k):
        at = pl.ds(k * rows_l, rows_l)
        return (
            pltpu.make_async_copy(act_hbm.at[at], act_buf.at[k % slots], l_sem.at[2 * (k % slots)]),
            pltpu.make_async_copy(grad_hbm.at[at], grad_buf.at[k % slots], l_sem.at[2 * (k % slots) + 1]),
        )

    load_pact = pltpu.make_async_copy(pact_hbm, pact, w_sem.at[0])
    load_pout = pltpu.make_async_copy(pout_hbm, pout, w_sem.at[1])
    load_pact.start()
    load_pout.start()
    for k in range(AHEAD):
        for c in load(k):
            c.start()
    lax.fori_loop(1, devices, greet, 0)
    stat_acc[...] = jnp.zeros_like(stat_acc)

    per_part = rows_l // SEQ
    parts_c = PARTS // CHUNKS

    def project(k):
        loads = load(k)
        if k == 0:
            load_pact.wait()
            load_pout.wait()
        for c in loads:
            c.wait()
        if k + AHEAD < PARTS and AHEAD < slots:
            for c in load(k + AHEAD):
                c.start()
        a_low = jnp.dot(
            act_buf[k % slots], pact[...], preferred_element_type=jnp.float32
        ).astype(jnp.bfloat16)
        g_low = jnp.dot(
            grad_buf[k % slots], pout[...], preferred_element_type=jnp.float32
        ).astype(jnp.bfloat16)
        if k + AHEAD < PARTS and AHEAD == slots:
            for c in load(k + AHEAD):
                c.start()
        for e in range(per_part):
            here = slice(e * SEQ, (e + 1) * SEQ)
            product = lax.dot_general(
                a_low[here], g_low[here], TN, preferred_element_type=jnp.float32)
            at = (k % parts_c) * per_part + e
            for h in range(wide.shape[0]):
                wide[h, pl.ds(at, a_low.shape[1], stride=ex_c), :] = (
                    product[:, h * 128:(h + 1) * 128])

    def narrow(chunk, slot):
        squares = jnp.zeros((8, 128), jnp.float32)
        for r in range(ranks):
            rows = pl.ds(pl.multiple_of((slot * ranks + r) * ex_c, ex_c), ex_c)
            for h in range(wide.shape[0]):
                low = wide[h, rows, :].astype(jnp.bfloat16)
                feat[chunk, slot, r, :, h * 128:(h + 1) * 128] = low
                back = low.astype(jnp.float32)
                squares += jnp.sum((back * back).reshape(ex_c // 8, 8, 128), axis=0)
        stat_acc[...] += squares

    def landing(chunk, pp):
        at = (seen_from(plane, pp) * groups + grp) * 2 + core
        return recv.at[:, pl.ds(pl.multiple_of(chunk * unit + at * ex_c, ex_c), ex_c), :]

    def either(side, pp, pc, local, remote):
        mine = jnp.logical_and(side * far_end == grp, 2 * pp + pc == blk)
        pl.when(mine)(local)
        pl.when(jnp.logical_not(mine))(remote)

    def send_stat(d, c):
        side, pp, pc = target_of(d)

        def local():
            pltpu.make_async_copy(stat_row, stats.at[me], t_recv).start()

        def remote():
            pltpu.make_async_remote_copy(
                src_ref=stat_row, dst_ref=stats.at[me], send_sem=t_send, recv_sem=t_recv,
                device_id=(side * far_end, 2 * pp + pc), device_id_type=MESH).start()

        either(side, pp, pc, local, remote)
        return c

    for chunk in range(CHUNKS):
        for k in range(parts_c):
            project(chunk * parts_c + k)
        if chunk == 0:
            pl.semaphore_wait(barrier, devices - 1)

        last_chunk = chunk == CHUNKS - 1
        if last_chunk:
            def settle_slot(slot, c, chunk=chunk):
                narrow(chunk, slot)
                return c

            lax.fori_loop(0, targets, settle_slot, 0)
            stat_row[...] = jnp.sum(stat_acc[...], axis=0, keepdims=True)
            lax.fori_loop(0, targets, send_stat, 0)

        def send(d, c, chunk=chunk, last_chunk=last_chunk):
            side, pp, pc = target_of(d)
            slot = (2 * pp + side) * 2 + pc
            if not last_chunk:
                narrow(chunk, slot)
            dst = landing(chunk, pp)

            def local():
                pltpu.make_async_copy(feat.at[chunk, slot], dst, f_recv.at[chunk]).start()

            def remote():
                pltpu.make_async_remote_copy(
                    src_ref=feat.at[chunk, slot], dst_ref=dst,
                    send_sem=f_send.at[chunk], recv_sem=f_recv.at[chunk],
                    device_id=(side * far_end, 2 * pp + pc), device_id_type=MESH).start()

            either(side, pp, pc, local, remote)
            return c

        lax.fori_loop(0, targets, send, 0)

    ones = jnp.ones((8, span), jnp.bfloat16)
    norm = 1.0 / math.sqrt(width)
    partner = (grp, blk + 1 - 2 * core)
    pieces = [(q, pc, ch) for q in range(planes) for pc in range(2) for ch in range(CHUNKS)]

    def nt(x, y):
        return lax.dot_general(x, y, NT, preferred_element_type=jnp.float32)

    def halves(v):
        high = v.astype(jnp.bfloat16)
        return high, (v - high.astype(jnp.float32)).astype(jnp.bfloat16)

    def arrive(u):
        rows = recv.at[:, pl.ds(u * unit, unit), :]
        pltpu.make_async_copy(rows, rows, f_recv.at[u]).wait()

    def over_ranks(left, right):
        total = None
        for r in range(ranks):
            term = nt(left(r), recv[r, right, :])
            total = term if total is None else total + term
        return total

    def area(u, v):
        return slice(u * unit, (u + 1) * unit), slice(v * unit, (v + 1) * unit)

    def tile_copy(u, v):
        t = TILES.index((u, v))
        a, b = area(u, v)
        return pltpu.make_async_remote_copy(
            src_ref=full.at[a, b], dst_ref=land.at[t],
            send_sem=k_send.at[t], recv_sem=k_recv.at[t],
            device_id=partner, device_id_type=MESH)

    def prow_copy():
        return pltpu.make_async_remote_copy(
            src_ref=prow_part, dst_ref=prow_land, send_sem=p_send, recv_sem=p_recv,
            device_id=partner, device_id_type=MESH)

    def rel_row(group, q, pc, ch):
        return ch * unit + ((seen_from(q, plane) * groups + group) * 2 + pc) * ex_c

    step_sq = min(256, unit)

    def squares_of(u, v):
        return [
            (slice(u * unit + i, u * unit + i + step_sq), slice(v * unit + j, v * unit + j + step_sq),
             slice(i, i + step_sq), slice(j, j + step_sq))
            for i in range(0, unit, step_sq) for j in range(0, unit, step_sq)]

    def own_work():
        def settle(u, v):
            tile_copy(u, v).wait_recv()
            tile_copy(u, v).wait_send()
            for a, b, i, j in squares_of(u, v):
                both = full[a, b] + land[TILES.index((u, v)), i, j]
                full[a, b] = both
                if keep:
                    w_high[a, b], w_low[a, b] = halves(both * shrink)
                if u != v:
                    both = both.T
                    full[b, a] = both
                    if keep:
                        w_high[b, a], w_low[b, a] = halves(both * shrink)

        for u in range(CHUNKS):
            arrive(u)
            for v in range(u + 1):
                for a, b, _, _ in squares_of(u, v):
                    full[a, b] = over_ranks(lambda r, a=a: recv[r, a, :], b)
                tile_copy(u, v).start()
            here = slice(u * unit, (u + 1) * unit)
            prow_part[:, here] = over_ranks(lambda r: ones, here)[:1] * norm
            if u == CHUNKS - 1:
                prow_copy().start()
            if u == 0:
                pltpu.make_async_copy(stats, stats, t_recv).wait()
                total = jnp.sum(jnp.sum(stats[...], axis=0), axis=1, keepdims=True)
                shrink = 1.0 / (total + 1e-30)
            for v in range(u + 1):
                settle(u, v)
        damping = damping_rate * total / (width * blocks)
        prow_copy().wait_recv()
        prow_copy().wait_send()

        row[...] = jnp.broadcast_to(prow_part[...] + prow_land[...], row.shape)

        def upright(values):
            for c in range(total_ex // 128):
                here = slice(c * 128, (c + 1) * 128)
                col[here, :] = jnp.broadcast_to(values[:, here], (128, 128)).T

        def image():
            def block_sum(i, total):
                for e in range(16):
                    rows = pl.ds(i * 128 + e * 8, 8)
                    weight = jnp.concatenate([col[rows, :]] * (total_ex // 128), axis=1)
                    total = total + full[rows, :] * weight
                return total

            start = jnp.zeros((8, total_ex), jnp.float32)
            if total_ex <= 512:
                for i in range(total_ex // 128):
                    start = block_sum(i, start)
            else:
                start = lax.fori_loop(
                    0, total_ex // 128,
                    lambda i, t: block_sum(i, t), start)
            return jnp.sum(start, axis=0, keepdims=True)

        step_ex = min(256, total_ex)

        def prepare(first):
            for n in range(batch):
                group = core * core_groups + first + n
                for m in range(0, len(pieces), 2):
                    at, to = rel_row(group, *pieces[m]), rel_row(group, *pieces[m + 1])
                    at, to = pl.multiple_of(at, ex_c), pl.multiple_of(to, ex_c)
                    y = jnp.concatenate(
                        [full[pl.ds(at, ex_c), :], full[pl.ds(to, ex_c), :]], axis=0) * shrink
                    here = slice(n * group_ex + m * ex_c, n * group_ex + (m + 2) * ex_c)
                    y_high[here, :], y_low[here, :] = halves(y)
                    lane = lax.broadcasted_iota(jnp.int32, (2 * ex_c, total_ex), 1)
                    sub = lax.broadcasted_iota(jnp.int32, (2 * ex_c, total_ex), 0)
                    spot = jnp.where(sub < ex_c, at + sub, to + sub - ex_c)
                    pick[here, :] = jnp.where(spot == lane, 1.0, 0.0).astype(jnp.bfloat16)

        def powers(at, fresh):
            yh, yl = y_high[...], y_low[...]
            if keep:
                wh, wl = w_high[at, :], w_low[at, :]
            else:
                wh, wl = halves(full[at, :] * shrink)
            vh, vl = halves(nt(yh, wh) + (nt(yh, wl) + nt(yl, wh)))
            for n in range(batch):
                here = slice(n * group_ex, (n + 1) * group_ex)
                ah, al, ph = y_high[here, at], y_low[here, at], pick[here, at]
                bh, bl = vh[here], vl[here]
                right = jnp.concatenate([ah, ph], axis=0)
                one = nt(ah, right) + nt(al, right)
                one_low = nt(ah, al)
                both_h = jnp.concatenate([ah, bh], axis=0)
                both_l = jnp.concatenate([al, bl], axis=0)
                two = nt(bh, both_h) + (nt(bh, both_l) + nt(bl, both_h))
                terms = (one[:, group_ex:], one[:, :group_ex] + one_low,
                         two[:, :group_ex], two[:, group_ex:])
                for k, term in enumerate(terms):
                    acc[n, k] = term if fresh else acc[n, k] + term

        def multiply():
            if total_ex <= 512:
                for k in range(total_ex // step_ex):
                    powers(slice(k * step_ex, (k + 1) * step_ex), k == 0)
            else:
                acc[...] = jnp.zeros_like(acc)

                def one_step(k, c):
                    powers(pl.ds(pl.multiple_of(k * step_ex, step_ex), step_ex), False)
                    return c

                lax.fori_loop(0, total_ex // step_ex, one_step, 0)

        prepare(0)
        multiply()
        values = row[:1, :]
        top = None
        for step in range(power_steps):
            upright(values)
            q = image()
            square = jnp.sum(values * q, axis=1, keepdims=True)
            top = jnp.sqrt(jnp.maximum(square, 0.0) + 1e-06)
            values = q / top

        center = damping + top
        rho, delta = top / center, damping / center
        zero, one = jnp.zeros_like(center), jnp.ones_like(center)

        def shifted(p):
            low = [delta * v for v in p] + [zero]
            return [a + b for a, b in zip(low, [zero] + list(p))]

        def plus(p, q, factor):
            n = max(len(p), len(q))
            p = list(p) + [zero] * (n - len(p))
            q = list(q) + [zero] * (n - len(q))
            return [a + factor * b for a, b in zip(p, q)]

        sig = one
        direction = [one]
        solution_poly = [one]
        residual = plus([one], shifted(direction), -sig)
        for sweep in range(1, ITERS):
            momentum = 0.5 * (rho * sig) ** 2 if sweep == 1 else (0.5 * rho * sig) ** 2
            sig = 1.0 / (1.0 - momentum / sig)
            direction = plus(residual, direction, momentum)
            solution_poly = plus(solution_poly, direction, sig)
            if sweep + 1 < ITERS:
                residual = plus(residual, shifted(direction), -sig)
        stretch = (total + 1e-30) / center
        factors = []
        power = stretch
        for coefficient in solution_poly:
            factors.append(coefficient * power)
            power = power * stretch

        for first in range(0, core_groups, batch):
            if first:
                prepare(first)
                multiply()
            for n in range(batch):
                score = factors[0] * acc[n, 0]
                for k in range(1, ITERS):
                    score = score + factors[k] * acc[n, k]
                sc[first + n] = score

        def send_score(d, c):
            b = 2 * lax.div(d, 2 * core_groups) + lax.rem(d, 2)
            n = lax.rem(lax.div(d, 2), core_groups)
            group = core * core_groups + n
            src = sc.at[n, pl.ds(pl.multiple_of(b * examples, examples), examples)]
            mine = jnp.logical_and(group == grp, b == blk)

            @pl.when(mine)
            def _():
                pltpu.make_async_copy(src, sc_land.at[block], o_recv.at[block]).start()

            @pl.when(jnp.logical_not(mine))
            def _():
                pltpu.make_async_remote_copy(
                    src_ref=src, dst_ref=sc_land.at[block],
                    send_sem=o_send.at[n * blocks + b], recv_sem=o_recv.at[block],
                    device_id=(group, b), device_id_type=MESH).start()

            return c

        lax.fori_loop(0, core_groups * blocks, send_score, 0)

    pl.when(is_owner)(own_work)

    def score_arrive(k, c):
        pltpu.make_async_copy(sc_land.at[k], sc_land.at[k], o_recv.at[k]).wait()
        return c

    lax.fori_loop(0, blocks, score_arrive, 0)
    out_ref[...] = jnp.sum(sc_land[...], axis=0)

    def gone(count):
        for chunk in range(CHUNKS):
            sent = feat.at[chunk, pl.ds(0, count)]
            pltpu.make_async_copy(sent, sent, f_send.at[chunk]).wait()
        rows = stats.at[pl.ds(0, count)]
        pltpu.make_async_copy(rows, rows, t_send).wait()

    @pl.when(is_owner)
    def _():
        gone(targets - 1)
        for n in range(core_groups):
            def score_gone(d, c, n=n):
                b = lax.rem(blk + d, blocks)
                group = core * core_groups + n
                src = sc.at[n, pl.ds(pl.multiple_of(b * examples, examples), examples)]

                @pl.when(jnp.logical_not(jnp.logical_and(group == grp, b == blk)))
                def _():
                    pltpu.make_async_copy(src, src, o_send.at[n * blocks + b]).wait()

                return c

            lax.fori_loop(0, blocks, score_gone, 0)

    @pl.when(jnp.logical_not(is_owner))
    def _():
        gone(targets)


def shards(groups, blocks, activations, out_grads, proj_act, proj_out):
    tokens, depth = activations.shape
    examples = tokens // SEQ
    rank, span = proj_act.shape[1], proj_out.shape[1]
    devices, targets = groups * blocks, 2 * blocks
    group_ex, total_ex = examples * blocks, examples * devices
    ranks = rank // targets
    width = rank * span // blocks
    unit = total_ex // CHUNKS
    ex_c, rows_l = examples // CHUNKS, tokens // PARTS
    small = total_ex <= 1024
    slots = PARTS if small else AHEAD
    batch = groups // 2 if small else 1
    split = total_ex if small else 8
    vmem = pl.BlockSpec(memory_space=pltpu.VMEM)
    hbm = pl.BlockSpec(memory_space=pl.ANY)
    f32, low = jnp.float32, jnp.bfloat16
    dma = pltpu.SemaphoreType.DMA
    tiles = len(TILES)
    scores = pl.pallas_call(
        functools.partial(mix_kernel, groups, blocks, examples, ranks, width, slots, batch, small),
        out_shape=jax.ShapeDtypeStruct((examples, group_ex), f32),
        in_specs=[hbm] * 4,
        out_specs=vmem,
        scratch_shapes=[
            pltpu.VMEM((slots, rows_l, depth), low),
            pltpu.VMEM((slots, rows_l, depth), low),
            pltpu.VMEM((depth, rank), low),
            pltpu.VMEM((depth, span), low),
            pltpu.VMEM((span // 128, rank * ex_c, 128), f32),
            pltpu.VMEM((CHUNKS, targets, ranks, ex_c, span), low),
            pltpu.VMEM((ranks, total_ex, span), low),
            pltpu.VMEM((8, 128), f32),
            pltpu.VMEM((1, 128), f32),
            pltpu.VMEM((devices, 1, 128), f32),
            pltpu.VMEM((tiles, unit, unit), f32),
            pltpu.VMEM((total_ex, total_ex), f32),
            pltpu.VMEM((split, total_ex), low),
            pltpu.VMEM((split, total_ex), low),
            pltpu.VMEM((1, total_ex), f32),
            pltpu.VMEM((1, total_ex), f32),
            pltpu.VMEM((8, total_ex), f32),
            pltpu.VMEM((total_ex, 128), f32),
            pltpu.VMEM((batch * group_ex, total_ex), low),
            pltpu.VMEM((batch * group_ex, total_ex), low),
            pltpu.VMEM((batch * group_ex, total_ex), low),
            pltpu.VMEM((batch, ITERS, group_ex, group_ex), f32),
            pltpu.VMEM((groups // 2, group_ex, group_ex), f32),
            pltpu.VMEM((blocks, examples, group_ex), f32),
            dma((2 * slots,)), dma((2,)), dma((CHUNKS,)), dma((CHUNKS,)), dma, dma,
            dma((tiles,)), dma((tiles,)), dma, dma,
            dma((groups // 2 * blocks,)), dma((blocks,)),
        ],
        compiler_params=pltpu.CompilerParams(
            collective_id=0, has_side_effects=True, vmem_limit_bytes=67043328
        ),
    )(activations, out_grads, proj_act, proj_out)
    return scores * float(examples * groups)


def solution(mesh):
    in_specs = (P(("grp", "blk"), None), P(("grp", "blk"), None), P(), P())
    out_specs = P(("grp", "blk"), None)
    body = functools.partial(shards, mesh.shape["grp"], mesh.shape["blk"])
    return jax.shard_map(body, mesh=mesh, in_specs=in_specs, out_specs=out_specs, check_vma=False)
```

```python
import functools
import math

import jax
import jax.numpy as jnp
from jax import lax
from jax.experimental import pallas as pl
from jax.experimental.pallas import tpu as pltpu
from jax.sharding import PartitionSpec as P

SEQ = 64
ITERS = 4
damping_rate = 0.5
power_steps = 3
CHUNKS = 2
PARTS = 4
AHEAD = 2
MESH = pl.DeviceIdType.MESH
NT = (((1,), (1,)), ((), ()))
TN = (((0,), (0,)), ((), ()))
TILES = [(i, j) for i in range(CHUNKS) for j in range(i + 1)]


def mix_kernel(
    groups, blocks, examples, ranks, width, slots, batch, keep,
    act_hbm, grad_hbm, pact_hbm, pout_hbm, out_ref,
    act_buf, grad_buf, pact, pout, wide, feat, recv, stat_acc, stat_row, stats,
    land, full, w_high, w_low, prow_part, prow_land, row, col, y_high, y_low, pick, acc, sc, sc_land,
    l_sem, w_sem, f_send, f_recv, t_send, t_recv, k_send, k_recv, p_send, p_recv, o_send, o_recv,
):
    devices = groups * blocks
    planes = blocks // 2
    far = planes // 2
    targets = 2 * blocks
    group_ex = examples * blocks
    total_ex = group_ex * groups
    unit = total_ex // CHUNKS
    span = recv.shape[2]
    ex_c = examples // CHUNKS
    core_groups = groups // 2
    grp, blk = lax.axis_index("grp"), lax.axis_index("blk")
    me = grp * blocks + blk
    core, plane = lax.rem(blk, 2), lax.div(blk, 2)
    sign = 1 - 2 * lax.rem(plane, 2)
    far_end = groups - 1
    is_owner = lax.rem(grp, far_end) == 0
    block = 2 * plane + lax.div(grp, far_end)

    def plane_at(rel):
        return lax.rem(plane + sign * rel + planes, planes)

    def seen_from(source, target):
        flip = 1 - 2 * lax.rem(target, 2)
        return lax.rem((source - target) * flip + planes, planes)

    def target_of(d):
        n = lax.div(d, 4)
        rel = lax.rem(far - n + planes, planes)
        j = lax.rem(d, 4)
        side = lax.rem(grp + lax.div(j, 2), 2)
        pc = lax.rem(core + lax.rem(j, 2), 2)
        return side, plane_at(rel), pc

    barrier = pltpu.get_barrier_semaphore()

    def greet(d, c):
        peer = lax.rem(me + d, devices)
        pl.semaphore_signal(
            barrier, inc=1, device_id=(lax.div(peer, blocks), lax.rem(peer, blocks)),
            device_id_type=MESH)
        return c

    rows_l = act_buf.shape[1]

    def load(k):
        at = pl.ds(k * rows_l, rows_l)
        return (
            pltpu.make_async_copy(act_hbm.at[at], act_buf.at[k % slots], l_sem.at[2 * (k % slots)]),
            pltpu.make_async_copy(grad_hbm.at[at], grad_buf.at[k % slots], l_sem.at[2 * (k % slots) + 1]),
        )

    load_pact = pltpu.make_async_copy(pact_hbm, pact, w_sem.at[0])
    load_pout = pltpu.make_async_copy(pout_hbm, pout, w_sem.at[1])
    load_pact.start()
    load_pout.start()
    for k in range(AHEAD):
        for c in load(k):
            c.start()
    lax.fori_loop(1, devices, greet, 0)
    stat_acc[...] = jnp.zeros_like(stat_acc)

    per_part = rows_l // SEQ
    parts_c = PARTS // CHUNKS

    def project(k):
        loads = load(k)
        if k == 0:
            load_pact.wait()
            load_pout.wait()
        for c in loads:
            c.wait()
        if k + AHEAD < PARTS and AHEAD < slots:
            for c in load(k + AHEAD):
                c.start()
        a_low = jnp.dot(
            act_buf[k % slots], pact[...], preferred_element_type=jnp.float32
        ).astype(jnp.bfloat16)
        g_low = jnp.dot(
            grad_buf[k % slots], pout[...], preferred_element_type=jnp.float32
        ).astype(jnp.bfloat16)
        if k + AHEAD < PARTS and AHEAD == slots:
            for c in load(k + AHEAD):
                c.start()
        for e in range(per_part):
            here = slice(e * SEQ, (e + 1) * SEQ)
            product = lax.dot_general(
                a_low[here], g_low[here], TN, preferred_element_type=jnp.float32)
            at = (k % parts_c) * per_part + e
            for h in range(wide.shape[0]):
                wide[h, pl.ds(at, a_low.shape[1], stride=ex_c), :] = (
                    product[:, h * 128:(h + 1) * 128])

    def narrow(chunk, slot):
        squares = jnp.zeros((8, 128), jnp.float32)
        for r in range(ranks):
            rows = pl.ds(pl.multiple_of((slot * ranks + r) * ex_c, ex_c), ex_c)
            for h in range(wide.shape[0]):
                low = wide[h, rows, :].astype(jnp.bfloat16)
                feat[chunk, slot, r, :, h * 128:(h + 1) * 128] = low
                back = low.astype(jnp.float32)
                squares += jnp.sum((back * back).reshape(ex_c // 8, 8, 128), axis=0)
        stat_acc[...] += squares

    def landing(chunk, pp):
        at = (seen_from(plane, pp) * groups + grp) * 2 + core
        return recv.at[:, pl.ds(pl.multiple_of(chunk * unit + at * ex_c, ex_c), ex_c), :]

    def either(side, pp, pc, local, remote):
        mine = jnp.logical_and(side * far_end == grp, 2 * pp + pc == blk)
        pl.when(mine)(local)
        pl.when(jnp.logical_not(mine))(remote)

    def send_stat(d, c):
        side, pp, pc = target_of(d)

        def local():
            pltpu.make_async_copy(stat_row, stats.at[me], t_recv).start()

        def remote():
            pltpu.make_async_remote_copy(
                src_ref=stat_row, dst_ref=stats.at[me], send_sem=t_send, recv_sem=t_recv,
                device_id=(side * far_end, 2 * pp + pc), device_id_type=MESH).start()

        either(side, pp, pc, local, remote)
        return c

    for chunk in range(CHUNKS):
        for k in range(parts_c):
            project(chunk * parts_c + k)
        if chunk == 0:
            pl.semaphore_wait(barrier, devices - 1)

        last_chunk = chunk == CHUNKS - 1
        if last_chunk:
            def settle_slot(slot, c, chunk=chunk):
                narrow(chunk, slot)
                return c

            lax.fori_loop(0, targets, settle_slot, 0)
            stat_row[...] = jnp.sum(stat_acc[...], axis=0, keepdims=True)
            lax.fori_loop(0, targets, send_stat, 0)

        def send(d, c, chunk=chunk, last_chunk=last_chunk):
            side, pp, pc = target_of(d)
            slot = (2 * pp + side) * 2 + pc
            if not last_chunk:
                narrow(chunk, slot)
            dst = landing(chunk, pp)

            def local():
                pltpu.make_async_copy(feat.at[chunk, slot], dst, f_recv.at[chunk]).start()

            def remote():
                pltpu.make_async_remote_copy(
                    src_ref=feat.at[chunk, slot], dst_ref=dst,
                    send_sem=f_send.at[chunk], recv_sem=f_recv.at[chunk],
                    device_id=(side * far_end, 2 * pp + pc), device_id_type=MESH).start()

            either(side, pp, pc, local, remote)
            return c

        lax.fori_loop(0, targets, send, 0)

    ones = jnp.ones((8, span), jnp.bfloat16)
    norm = 1.0 / math.sqrt(width)
    partner = (grp, blk + 1 - 2 * core)
    pieces = [(q, pc, ch) for q in range(planes) for pc in range(2) for ch in range(CHUNKS)]

    def nt(x, y):
        return lax.dot_general(x, y, NT, preferred_element_type=jnp.float32)

    def halves(v):
        high = v.astype(jnp.bfloat16)
        return high, (v - high.astype(jnp.float32)).astype(jnp.bfloat16)

    def arrive(u):
        rows = recv.at[:, pl.ds(u * unit, unit), :]
        pltpu.make_async_copy(rows, rows, f_recv.at[u]).wait()

    def over_ranks(left, right):
        total = None
        for r in range(ranks):
            term = nt(left(r), recv[r, right, :])
            total = term if total is None else total + term
        return total

    def area(u, v):
        return slice(u * unit, (u + 1) * unit), slice(v * unit, (v + 1) * unit)

    def tile_copy(u, v):
        t = TILES.index((u, v))
        a, b = area(u, v)
        return pltpu.make_async_remote_copy(
            src_ref=full.at[a, b], dst_ref=land.at[t],
            send_sem=k_send.at[t], recv_sem=k_recv.at[t],
            device_id=partner, device_id_type=MESH)

    def prow_copy():
        return pltpu.make_async_remote_copy(
            src_ref=prow_part, dst_ref=prow_land, send_sem=p_send, recv_sem=p_recv,
            device_id=partner, device_id_type=MESH)

    def rel_row(group, q, pc, ch):
        return ch * unit + ((seen_from(q, plane) * groups + group) * 2 + pc) * ex_c

    step_sq = min(256, unit)

    def squares_of(u, v):
        return [
            (slice(u * unit + i, u * unit + i + step_sq), slice(v * unit + j, v * unit + j + step_sq),
             slice(i, i + step_sq), slice(j, j + step_sq))
            for i in range(0, unit, step_sq) for j in range(0, unit, step_sq)]

    def own_work():
        def settle(u, v):
            tile_copy(u, v).wait_recv()
            tile_copy(u, v).wait_send()
            for a, b, i, j in squares_of(u, v):
                both = full[a, b] + land[TILES.index((u, v)), i, j]
                full[a, b] = both
                if keep:
                    w_high[a, b], w_low[a, b] = halves(both * shrink)
                if u != v:
                    both = both.T
                    full[b, a] = both
                    if keep:
                        w_high[b, a], w_low[b, a] = halves(both * shrink)

        for u in range(CHUNKS):
            arrive(u)
            for v in range(u + 1):
                for a, b, _, _ in squares_of(u, v):
                    full[a, b] = over_ranks(lambda r, a=a: recv[r, a, :], b)
                tile_copy(u, v).start()
            here = slice(u * unit, (u + 1) * unit)
            prow_part[:, here] = over_ranks(lambda r: ones, here)[:1] * norm
            if u == CHUNKS - 1:
                prow_copy().start()
            if u == 0:
                pltpu.make_async_copy(stats, stats, t_recv).wait()
                total = jnp.sum(jnp.sum(stats[...], axis=0), axis=1, keepdims=True)
                shrink = 1.0 / (total + 1e-30)
            for v in range(u + 1):
                settle(u, v)
        damping = damping_rate * total / (width * blocks)
        prow_copy().wait_recv()
        prow_copy().wait_send()

        row[...] = jnp.broadcast_to(prow_part[...] + prow_land[...], row.shape)

        def upright(values):
            for c in range(total_ex // 128):
                here = slice(c * 128, (c + 1) * 128)
                col[here, :] = jnp.broadcast_to(values[:, here], (128, 128)).T

        def image():
            def block_sum(i, total):
                for e in range(16):
                    rows = pl.ds(i * 128 + e * 8, 8)
                    weight = jnp.concatenate([col[rows, :]] * (total_ex // 128), axis=1)
                    total = total + full[rows, :] * weight
                return total

            start = jnp.zeros((8, total_ex), jnp.float32)
            if total_ex <= 512:
                for i in range(total_ex // 128):
                    start = block_sum(i, start)
            else:
                start = lax.fori_loop(
                    0, total_ex // 128,
                    lambda i, t: block_sum(i, t), start)
            return jnp.sum(start, axis=0, keepdims=True)

        step_ex = min(256, total_ex)

        def prepare(first):
            for n in range(batch):
                group = core * core_groups + first + n
                for m in range(0, len(pieces), 2):
                    at, to = rel_row(group, *pieces[m]), rel_row(group, *pieces[m + 1])
                    at, to = pl.multiple_of(at, ex_c), pl.multiple_of(to, ex_c)
                    y = jnp.concatenate(
                        [full[pl.ds(at, ex_c), :], full[pl.ds(to, ex_c), :]], axis=0) * shrink
                    here = slice(n * group_ex + m * ex_c, n * group_ex + (m + 2) * ex_c)
                    y_high[here, :], y_low[here, :] = halves(y)
                    lane = lax.broadcasted_iota(jnp.int32, (2 * ex_c, total_ex), 1)
                    sub = lax.broadcasted_iota(jnp.int32, (2 * ex_c, total_ex), 0)
                    spot = jnp.where(sub < ex_c, at + sub, to + sub - ex_c)
                    pick[here, :] = jnp.where(spot == lane, 1.0, 0.0).astype(jnp.bfloat16)

        def powers(at, fresh):
            yh, yl = y_high[...], y_low[...]
            if keep:
                wh, wl = w_high[at, :], w_low[at, :]
            else:
                wh, wl = halves(full[at, :] * shrink)
            vh, vl = halves(nt(yh, wh) + (nt(yh, wl) + nt(yl, wh)))
            for n in range(batch):
                here = slice(n * group_ex, (n + 1) * group_ex)
                ah, al, ph = y_high[here, at], y_low[here, at], pick[here, at]
                bh, bl = vh[here], vl[here]
                right = jnp.concatenate([ah, ph], axis=0)
                one = nt(ah, right) + nt(al, right)
                one_low = nt(ah, al)
                both_h = jnp.concatenate([ah, bh], axis=0)
                both_l = jnp.concatenate([al, bl], axis=0)
                two = nt(bh, both_h) + (nt(bh, both_l) + nt(bl, both_h))
                terms = (one[:, group_ex:], one[:, :group_ex] + one_low,
                         two[:, :group_ex], two[:, group_ex:])
                for k, term in enumerate(terms):
                    acc[n, k] = term if fresh else acc[n, k] + term

        def multiply():
            if total_ex <= 512:
                for k in range(total_ex // step_ex):
                    powers(slice(k * step_ex, (k + 1) * step_ex), k == 0)
            else:
                acc[...] = jnp.zeros_like(acc)

                def one_step(k, c):
                    powers(pl.ds(pl.multiple_of(k * step_ex, step_ex), step_ex), False)
                    return c

                lax.fori_loop(0, total_ex // step_ex, one_step, 0)

        prepare(0)
        multiply()
        values = row[:1, :]
        top = None
        for step in range(power_steps):
            upright(values)
            q = image()
            square = jnp.sum(values * q, axis=1, keepdims=True)
            top = jnp.sqrt(jnp.maximum(square, 0.0) + 1e-06)
            values = q / top

        center = damping + top
        rho, delta = top / center, damping / center
        zero, one = jnp.zeros_like(center), jnp.ones_like(center)

        def shifted(p):
            low = [delta * v for v in p] + [zero]
            return [a + b for a, b in zip(low, [zero] + list(p))]

        def plus(p, q, factor):
            n = max(len(p), len(q))
            p = list(p) + [zero] * (n - len(p))
            q = list(q) + [zero] * (n - len(q))
            return [a + factor * b for a, b in zip(p, q)]

        sig = one
        direction = [one]
        solution_poly = [one]
        residual = plus([one], shifted(direction), -sig)
        for sweep in range(1, ITERS):
            momentum = 0.5 * (rho * sig) ** 2 if sweep == 1 else (0.5 * rho * sig) ** 2
            sig = 1.0 / (1.0 - momentum / sig)
            direction = plus(residual, direction, momentum)
            solution_poly = plus(solution_poly, direction, sig)
            if sweep + 1 < ITERS:
                residual = plus(residual, shifted(direction), -sig)
        stretch = (total + 1e-30) / center
        factors = []
        power = stretch
        for coefficient in solution_poly:
            factors.append(coefficient * power)
            power = power * stretch

        for first in range(0, core_groups, batch):
            if first:
                prepare(first)
                multiply()
            for n in range(batch):
                score = factors[0] * acc[n, 0]
                for k in range(1, ITERS):
                    score = score + factors[k] * acc[n, k]
                sc[first + n] = score

        def send_score(d, c):
            b = 2 * lax.div(d, 2 * core_groups) + lax.rem(d, 2)
            n = lax.rem(lax.div(d, 2), core_groups)
            group = core * core_groups + n
            src = sc.at[n, pl.ds(pl.multiple_of(b * examples, examples), examples)]
            mine = jnp.logical_and(group == grp, b == blk)

            @pl.when(mine)
            def _():
                pltpu.make_async_copy(src, sc_land.at[block], o_recv.at[block]).start()

            @pl.when(jnp.logical_not(mine))
            def _():
                pltpu.make_async_remote_copy(
                    src_ref=src, dst_ref=sc_land.at[block],
                    send_sem=o_send.at[n * blocks + b], recv_sem=o_recv.at[block],
                    device_id=(group, b), device_id_type=MESH).start()

            return c

        lax.fori_loop(0, core_groups * blocks, send_score, 0)

    pl.when(is_owner)(own_work)

    def score_arrive(k, c):
        pltpu.make_async_copy(sc_land.at[k], sc_land.at[k], o_recv.at[k]).wait()
        return c

    lax.fori_loop(0, blocks, score_arrive, 0)
    out_ref[...] = jnp.sum(sc_land[...], axis=0)

    def gone(count):
        for chunk in range(CHUNKS):
            sent = feat.at[chunk, pl.ds(0, count)]
            pltpu.make_async_copy(sent, sent, f_send.at[chunk]).wait()
        rows = stats.at[pl.ds(0, count)]
        pltpu.make_async_copy(rows, rows, t_send).wait()

    @pl.when(is_owner)
    def _():
        gone(targets - 1)
        for n in range(core_groups):
            def score_gone(d, c, n=n):
                b = lax.rem(blk + d, blocks)
                group = core * core_groups + n
                src = sc.at[n, pl.ds(pl.multiple_of(b * examples, examples), examples)]

                @pl.when(jnp.logical_not(jnp.logical_and(group == grp, b == blk)))
                def _():
                    pltpu.make_async_copy(src, src, o_send.at[n * blocks + b]).wait()

                return c

            lax.fori_loop(0, blocks, score_gone, 0)

    @pl.when(jnp.logical_not(is_owner))
    def _():
        gone(targets)


def shards(groups, blocks, activations, out_grads, proj_act, proj_out):
    tokens, depth = activations.shape
    examples = tokens // SEQ
    rank, span = proj_act.shape[1], proj_out.shape[1]
    devices, targets = groups * blocks, 2 * blocks
    group_ex, total_ex = examples * blocks, examples * devices
    ranks = rank // targets
    width = rank * span // blocks
    unit = total_ex // CHUNKS
    ex_c, rows_l = examples // CHUNKS, tokens // PARTS
    small = total_ex <= 1024
    slots = PARTS if small else AHEAD
    batch = groups // 2 if small else 1
    split = total_ex if small else 8
    vmem = pl.BlockSpec(memory_space=pltpu.VMEM)
    hbm = pl.BlockSpec(memory_space=pl.ANY)
    f32, low = jnp.float32, jnp.bfloat16
    dma = pltpu.SemaphoreType.DMA
    tiles = len(TILES)
    scores = pl.pallas_call(
        functools.partial(mix_kernel, groups, blocks, examples, ranks, width, slots, batch, small),
        out_shape=jax.ShapeDtypeStruct((examples, group_ex), f32),
        in_specs=[hbm] * 4,
        out_specs=vmem,
        scratch_shapes=[
            pltpu.VMEM((slots, rows_l, depth), low),
            pltpu.VMEM((slots, rows_l, depth), low),
            pltpu.VMEM((depth, rank), low),
            pltpu.VMEM((depth, span), low),
            pltpu.VMEM((span // 128, rank * ex_c, 128), f32),
            pltpu.VMEM((CHUNKS, targets, ranks, ex_c, span), low),
            pltpu.VMEM((ranks, total_ex, span), low),
            pltpu.VMEM((8, 128), f32),
            pltpu.VMEM((1, 128), f32),
            pltpu.VMEM((devices, 1, 128), f32),
            pltpu.VMEM((tiles, unit, unit), f32),
            pltpu.VMEM((total_ex, total_ex), f32),
            pltpu.VMEM((split, total_ex), low),
            pltpu.VMEM((split, total_ex), low),
            pltpu.VMEM((1, total_ex), f32),
            pltpu.VMEM((1, total_ex), f32),
            pltpu.VMEM((8, total_ex), f32),
            pltpu.VMEM((total_ex, 128), f32),
            pltpu.VMEM((batch * group_ex, total_ex), low),
            pltpu.VMEM((batch * group_ex, total_ex), low),
            pltpu.VMEM((batch * group_ex, total_ex), low),
            pltpu.VMEM((batch, ITERS, group_ex, group_ex), f32),
            pltpu.VMEM((groups // 2, group_ex, group_ex), f32),
            pltpu.VMEM((blocks, examples, group_ex), f32),
            dma((2 * slots,)), dma((2,)), dma((CHUNKS,)), dma((CHUNKS,)), dma, dma,
            dma((tiles,)), dma((tiles,)), dma, dma,
            dma((groups // 2 * blocks,)), dma((blocks,)),
        ],
        compiler_params=pltpu.CompilerParams(
            collective_id=0, has_side_effects=True,
            vmem_limit_bytes=(40 << 20) if small else 67043328,
        ),
    )(*[pltpu.with_memory_space_constraint(v, pltpu.HBM)
        for v in (activations, out_grads, proj_act, proj_out)])
    return scores * float(examples * groups)


def solution(mesh):
    in_specs = (P(("grp", "blk"), None), P(("grp", "blk"), None), P(), P())
    out_specs = P(("grp", "blk"), None)
    body = functools.partial(shards, mesh.shape["grp"], mesh.shape["blk"])
    return jax.shard_map(body, mesh=mesh, in_specs=in_specs, out_specs=out_specs, check_vma=False)
```

```python
import functools
import math

import jax
import jax.numpy as jnp
from jax import lax
from jax.experimental import pallas as pl
from jax.experimental.pallas import tpu as pltpu
from jax.sharding import PartitionSpec as P

SEQ = 64
ITERS = 4
damping_rate = 0.5
power_steps = 3
CHUNKS = 2
PARTS = 4
AHEAD = 2
MESH = pl.DeviceIdType.MESH
NT = (((1,), (1,)), ((), ()))
TN = (((0,), (0,)), ((), ()))
TILES = [(i, j) for i in range(CHUNKS) for j in range(i + 1)]


def mix_kernel(
    groups, blocks, examples, ranks, width, slots, batch, keep,
    act_hbm, grad_hbm, pact_hbm, pout_hbm, out_ref,
    act_buf, grad_buf, pact, pout, wide, feat, recv, stat_acc, stat_row, stats,
    land, full, w_high, w_low, prow_part, prow_land, row, col, y_high, y_low, pick, acc, sc, sc_land,
    l_sem, w_sem, f_send, f_recv, t_send, t_recv, k_send, k_recv, p_send, p_recv, o_send, o_recv,
):
    devices = groups * blocks
    planes = blocks // 2
    far = planes // 2
    targets = 2 * blocks
    group_ex = examples * blocks
    total_ex = group_ex * groups
    unit = total_ex // CHUNKS
    span = recv.shape[2]
    ex_c = examples // CHUNKS
    core_groups = groups // 2
    grp, blk = lax.axis_index("grp"), lax.axis_index("blk")
    me = grp * blocks + blk
    core, plane = lax.rem(blk, 2), lax.div(blk, 2)
    sign = 1 - 2 * lax.rem(plane, 2)
    far_end = groups - 1
    is_owner = lax.rem(grp, far_end) == 0
    block = 2 * plane + lax.div(grp, far_end)

    def plane_at(rel):
        return lax.rem(plane + sign * rel + planes, planes)

    def seen_from(source, target):
        flip = 1 - 2 * lax.rem(target, 2)
        return lax.rem((source - target) * flip + planes, planes)

    def target_of(d):
        n = lax.div(d, 4)
        rel = lax.rem(far - n + planes, planes)
        j = lax.rem(d, 4)
        side = lax.rem(grp + lax.div(j, 2), 2)
        pc = lax.rem(core + lax.rem(j, 2), 2)
        return side, plane_at(rel), pc

    barrier = pltpu.get_barrier_semaphore()

    def greet(d, c):
        peer = lax.rem(me + d, devices)
        pl.semaphore_signal(
            barrier, inc=1, device_id=(lax.div(peer, blocks), lax.rem(peer, blocks)),
            device_id_type=MESH)
        return c

    rows_l = act_buf.shape[1]

    def load(k):
        at = pl.ds(k * rows_l, rows_l)
        return (
            pltpu.make_async_copy(act_hbm.at[at], act_buf.at[k % slots], l_sem.at[2 * (k % slots)]),
            pltpu.make_async_copy(grad_hbm.at[at], grad_buf.at[k % slots], l_sem.at[2 * (k % slots) + 1]),
        )

    load_pact = pltpu.make_async_copy(pact_hbm, pact, w_sem.at[0])
    load_pout = pltpu.make_async_copy(pout_hbm, pout, w_sem.at[1])
    load_pact.start()
    load_pout.start()
    for k in range(AHEAD):
        for c in load(k):
            c.start()
    lax.fori_loop(1, devices, greet, 0)
    stat_acc[...] = jnp.zeros_like(stat_acc)

    per_part = rows_l // SEQ
    parts_c = PARTS // CHUNKS

    def project(k):
        loads = load(k)
        if k == 0:
            load_pact.wait()
            load_pout.wait()
        for c in loads:
            c.wait()
        if k + AHEAD < PARTS and AHEAD < slots:
            for c in load(k + AHEAD):
                c.start()
        a_low = jnp.dot(
            act_buf[k % slots], pact[...], preferred_element_type=jnp.float32
        ).astype(jnp.bfloat16)
        g_low = jnp.dot(
            grad_buf[k % slots], pout[...], preferred_element_type=jnp.float32
        ).astype(jnp.bfloat16)
        if k + AHEAD < PARTS and AHEAD == slots:
            for c in load(k + AHEAD):
                c.start()
        for e in range(per_part):
            here = slice(e * SEQ, (e + 1) * SEQ)
            product = lax.dot_general(
                a_low[here], g_low[here], TN, preferred_element_type=jnp.float32)
            at = (k % parts_c) * per_part + e
            for h in range(wide.shape[0]):
                wide[h, pl.ds(at, a_low.shape[1], stride=ex_c), :] = (
                    product[:, h * 128:(h + 1) * 128])

    def narrow(chunk, slot):
        squares = jnp.zeros((8, 128), jnp.float32)
        for r in range(ranks):
            rows = pl.ds(pl.multiple_of((slot * ranks + r) * ex_c, ex_c), ex_c)
            for h in range(wide.shape[0]):
                low = wide[h, rows, :].astype(jnp.bfloat16)
                feat[chunk, slot, r, :, h * 128:(h + 1) * 128] = low
                back = low.astype(jnp.float32)
                squares += jnp.sum((back * back).reshape(ex_c // 8, 8, 128), axis=0)
        stat_acc[...] += squares

    def landing(chunk, pp):
        at = (seen_from(plane, pp) * groups + grp) * 2 + core
        return recv.at[:, pl.ds(pl.multiple_of(chunk * unit + at * ex_c, ex_c), ex_c), :]

    def either(side, pp, pc, local, remote):
        mine = jnp.logical_and(side * far_end == grp, 2 * pp + pc == blk)
        pl.when(mine)(local)
        pl.when(jnp.logical_not(mine))(remote)

    def send_stat(d, c):
        side, pp, pc = target_of(d)

        def local():
            pltpu.make_async_copy(stat_row, stats.at[me], t_recv).start()

        def remote():
            pltpu.make_async_remote_copy(
                src_ref=stat_row, dst_ref=stats.at[me], send_sem=t_send, recv_sem=t_recv,
                device_id=(side * far_end, 2 * pp + pc), device_id_type=MESH).start()

        either(side, pp, pc, local, remote)
        return c

    for chunk in range(CHUNKS):
        for k in range(parts_c):
            project(chunk * parts_c + k)
        if chunk == 0:
            pl.semaphore_wait(barrier, devices - 1)

        last_chunk = chunk == CHUNKS - 1
        if last_chunk:
            def settle_slot(slot, c, chunk=chunk):
                narrow(chunk, slot)
                return c

            lax.fori_loop(0, targets, settle_slot, 0)
            stat_row[...] = jnp.sum(stat_acc[...], axis=0, keepdims=True)
            lax.fori_loop(0, targets, send_stat, 0)

        def send(d, c, chunk=chunk, last_chunk=last_chunk):
            side, pp, pc = target_of(d)
            slot = (2 * pp + side) * 2 + pc
            if not last_chunk:
                narrow(chunk, slot)
            dst = landing(chunk, pp)

            def local():
                pltpu.make_async_copy(feat.at[chunk, slot], dst, f_recv.at[chunk]).start()

            def remote():
                pltpu.make_async_remote_copy(
                    src_ref=feat.at[chunk, slot], dst_ref=dst,
                    send_sem=f_send.at[chunk], recv_sem=f_recv.at[chunk],
                    device_id=(side * far_end, 2 * pp + pc), device_id_type=MESH).start()

            either(side, pp, pc, local, remote)
            return c

        lax.fori_loop(0, targets, send, 0)

    ones = jnp.ones((16, span), jnp.bfloat16)
    norm = 1.0 / math.sqrt(width)
    partner = (grp, blk + 1 - 2 * core)
    pieces = [(q, pc, ch) for q in range(planes) for pc in range(2) for ch in range(CHUNKS)]

    def nt(x, y):
        return lax.dot_general(x, y, NT, preferred_element_type=jnp.float32)

    def halves(v):
        high = v.astype(jnp.bfloat16)
        return high, (v - high.astype(jnp.float32)).astype(jnp.bfloat16)

    def arrive(u):
        rows = recv.at[:, pl.ds(u * unit, unit), :]
        pltpu.make_async_copy(rows, rows, f_recv.at[u]).wait()

    def over_ranks(left, right):
        total = None
        for r in range(ranks):
            term = nt(left(r), recv[r, right, :])
            total = term if total is None else total + term
        return total

    def area(u, v):
        return slice(u * unit, (u + 1) * unit), slice(v * unit, (v + 1) * unit)

    def tile_copy(u, v):
        t = TILES.index((u, v))
        a, b = area(u, v)
        return pltpu.make_async_remote_copy(
            src_ref=full.at[a, b], dst_ref=land.at[t],
            send_sem=k_send.at[t], recv_sem=k_recv.at[t],
            device_id=partner, device_id_type=MESH)

    def prow_copy():
        return pltpu.make_async_remote_copy(
            src_ref=prow_part, dst_ref=prow_land, send_sem=p_send, recv_sem=p_recv,
            device_id=partner, device_id_type=MESH)

    def rel_row(group, q, pc, ch):
        return ch * unit + ((seen_from(q, plane) * groups + group) * 2 + pc) * ex_c

    step_sq = min(256, unit)

    def squares_of(u, v):
        return [
            (slice(u * unit + i, u * unit + i + step_sq), slice(v * unit + j, v * unit + j + step_sq),
             slice(i, i + step_sq), slice(j, j + step_sq))
            for i in range(0, unit, step_sq) for j in range(0, unit, step_sq)]

    def own_work():
        def spots(first):
            for n in range(batch):
                group = core * core_groups + first + n
                for m in range(0, len(pieces), 2):
                    at, to = rel_row(group, *pieces[m]), rel_row(group, *pieces[m + 1])
                    here = slice(n * group_ex + m * ex_c, n * group_ex + (m + 2) * ex_c)
                    lane = lax.broadcasted_iota(jnp.int32, (2 * ex_c, total_ex), 1)
                    sub = lax.broadcasted_iota(jnp.int32, (2 * ex_c, total_ex), 0)
                    spot = jnp.where(sub < ex_c, at + sub, to + sub - ex_c)
                    pick[here, :] = jnp.where(spot == lane, 1.0, 0.0).astype(jnp.bfloat16)

        def gather(first):
            for n in range(batch):
                group = core * core_groups + first + n
                for m in range(0, len(pieces), 2):
                    at, to = rel_row(group, *pieces[m]), rel_row(group, *pieces[m + 1])
                    at, to = pl.multiple_of(at, ex_c), pl.multiple_of(to, ex_c)
                    y = jnp.concatenate(
                        [full[pl.ds(at, ex_c), :], full[pl.ds(to, ex_c), :]], axis=0) * shrink
                    here = slice(n * group_ex + m * ex_c, n * group_ex + (m + 2) * ex_c)
                    y_high[here, :], y_low[here, :] = halves(y)

        def settle(u, v):
            tile_copy(u, v).wait_recv()
            tile_copy(u, v).wait_send()
            for a, b, i, j in squares_of(u, v):
                both = full[a, b] + land[TILES.index((u, v)), i, j]
                full[a, b] = both
                if keep:
                    w_high[a, b], w_low[a, b] = halves(both * shrink)
                if u != v:
                    both = both.T
                    full[b, a] = both
                    if keep:
                        w_high[b, a], w_low[b, a] = halves(both * shrink)

        spots(0)
        for u in range(CHUNKS):
            arrive(u)
            for v in range(u + 1):
                for a, b, i, j in squares_of(u, v):
                    summed = u == v and i.start == 0

                    def left(r, a=a, summed=summed):
                        rows = recv[r, a, :]
                        return jnp.concatenate([rows, ones], axis=0) if summed else rows

                    found = over_ranks(left, b)
                    full[a, b] = found[:step_sq]
                    if summed:
                        prow_part[:, b] = found[step_sq:step_sq + 1] * norm
                tile_copy(u, v).start()
            if u == CHUNKS - 1:
                prow_copy().start()
            if u == 0:
                pltpu.make_async_copy(stats, stats, t_recv).wait()
                total = jnp.sum(jnp.sum(stats[...], axis=0), axis=1, keepdims=True)
                shrink = 1.0 / (total + 1e-30)
            for v in range(u + 1):
                settle(u, v)
        damping = damping_rate * total / (width * blocks)
        prow_copy().wait_recv()
        prow_copy().wait_send()

        row[...] = jnp.broadcast_to(prow_part[...] + prow_land[...], row.shape)

        def upright(values):
            for c in range(total_ex // 128):
                here = slice(c * 128, (c + 1) * 128)
                col[here, :] = jnp.broadcast_to(values[:, here], (128, 128)).T

        def image():
            def block_sum(i, total):
                for e in range(16):
                    rows = pl.ds(i * 128 + e * 8, 8)
                    weight = jnp.concatenate([col[rows, :]] * (total_ex // 128), axis=1)
                    total = total + full[rows, :] * weight
                return total

            start = jnp.zeros((8, total_ex), jnp.float32)
            if total_ex <= 512:
                for i in range(total_ex // 128):
                    start = block_sum(i, start)
            else:
                start = lax.fori_loop(
                    0, total_ex // 128,
                    lambda i, t: block_sum(i, t), start)
            return jnp.sum(start, axis=0, keepdims=True)

        step_ex = min(256, total_ex)

        def powers(at, fresh):
            yh, yl = y_high[...], y_low[...]
            if keep:
                wh, wl = w_high[at, :], w_low[at, :]
            else:
                wh, wl = halves(full[at, :] * shrink)
            count = yh.shape[0]
            stacked = nt(jnp.concatenate([yh, yl], axis=0), wh)
            vh, vl = halves(stacked[:count] + (stacked[count:] + nt(yh, wl)))
            g = group_ex
            for n in range(batch):
                here = slice(n * g, (n + 1) * g)
                ah, al, ph = y_high[here, at], y_low[here, at], pick[here, at]
                bh, bl = vh[here], vl[here]
                one = nt(jnp.concatenate([ah, al], axis=0), jnp.concatenate([ah, ph], axis=0))
                two = nt(jnp.concatenate([bh, bl], axis=0), jnp.concatenate([ah, bh], axis=0))
                low = nt(jnp.concatenate([ah, bh], axis=0), jnp.concatenate([al, bl], axis=0))
                terms = (one[:g, g:] + one[g:, g:],
                         one[:g, :g] + (one[g:, :g] + low[:g, :g]),
                         two[:g, :g] + (two[g:, :g] + low[g:, :g]),
                         two[:g, g:] + (two[g:, g:] + low[g:, g:]))
                for k, term in enumerate(terms):
                    acc[n, k] = term if fresh else acc[n, k] + term

        def multiply():
            if total_ex <= 512:
                for k in range(total_ex // step_ex):
                    powers(slice(k * step_ex, (k + 1) * step_ex), k == 0)
            else:
                acc[...] = jnp.zeros_like(acc)

                def one_step(k, c):
                    powers(pl.ds(pl.multiple_of(k * step_ex, step_ex), step_ex), False)
                    return c

                lax.fori_loop(0, total_ex // step_ex, one_step, 0)

        gather(0)
        multiply()
        values = row[:1, :]
        top = None
        for step in range(power_steps):
            upright(values)
            q = image()
            square = jnp.sum(values * q, axis=1, keepdims=True)
            top = jnp.sqrt(jnp.maximum(square, 0.0) + 1e-06)
            values = q / top

        center = damping + top
        rho, delta = top / center, damping / center
        zero, one = jnp.zeros_like(center), jnp.ones_like(center)

        def shifted(p):
            low = [delta * v for v in p] + [zero]
            return [a + b for a, b in zip(low, [zero] + list(p))]

        def plus(p, q, factor):
            n = max(len(p), len(q))
            p = list(p) + [zero] * (n - len(p))
            q = list(q) + [zero] * (n - len(q))
            return [a + factor * b for a, b in zip(p, q)]

        sig = one
        direction = [one]
        solution_poly = [one]
        residual = plus([one], shifted(direction), -sig)
        for sweep in range(1, ITERS):
            pull = (0.5 if sweep == 1 else 0.25) * rho * rho * sig
            momentum = pull * sig
            sig = 1.0 / (1.0 - pull)
            direction = plus(residual, direction, momentum)
            solution_poly = plus(solution_poly, direction, sig)
            if sweep + 1 < ITERS:
                residual = plus(residual, shifted(direction), -sig)
        stretch = (total + 1e-30) / center
        factors = []
        power = stretch
        for coefficient in solution_poly:
            factors.append(coefficient * power)
            power = power * stretch

        for first in range(0, core_groups, batch):
            if first:
                spots(first)
                gather(first)
                multiply()
            for n in range(batch):
                score = factors[0] * acc[n, 0]
                for k in range(1, ITERS):
                    score = score + factors[k] * acc[n, k]
                sc[first + n] = score

        def send_score(d, c):
            b = 2 * lax.div(d, 2 * core_groups) + lax.rem(d, 2)
            n = lax.rem(lax.div(d, 2), core_groups)
            group = core * core_groups + n
            src = sc.at[n, pl.ds(pl.multiple_of(b * examples, examples), examples)]
            mine = jnp.logical_and(group == grp, b == blk)

            @pl.when(mine)
            def _():
                pltpu.make_async_copy(src, sc_land.at[block], o_recv.at[block]).start()

            @pl.when(jnp.logical_not(mine))
            def _():
                pltpu.make_async_remote_copy(
                    src_ref=src, dst_ref=sc_land.at[block],
                    send_sem=o_send.at[n * blocks + b], recv_sem=o_recv.at[block],
                    device_id=(group, b), device_id_type=MESH).start()

            return c

        lax.fori_loop(0, core_groups * blocks, send_score, 0)

    pl.when(is_owner)(own_work)

    def score_arrive(k, c):
        pltpu.make_async_copy(sc_land.at[k], sc_land.at[k], o_recv.at[k]).wait()
        return c

    lax.fori_loop(0, blocks, score_arrive, 0)
    out_ref[...] = jnp.sum(sc_land[...], axis=0)

    def gone(count):
        for chunk in range(CHUNKS):
            sent = feat.at[chunk, pl.ds(0, count)]
            pltpu.make_async_copy(sent, sent, f_send.at[chunk]).wait()
        rows = stats.at[pl.ds(0, count)]
        pltpu.make_async_copy(rows, rows, t_send).wait()

    @pl.when(is_owner)
    def _():
        gone(targets - 1)
        for n in range(core_groups):
            def score_gone(d, c, n=n):
                b = lax.rem(blk + d, blocks)
                group = core * core_groups + n
                src = sc.at[n, pl.ds(pl.multiple_of(b * examples, examples), examples)]

                @pl.when(jnp.logical_not(jnp.logical_and(group == grp, b == blk)))
                def _():
                    pltpu.make_async_copy(src, src, o_send.at[n * blocks + b]).wait()

                return c

            lax.fori_loop(0, blocks, score_gone, 0)

    @pl.when(jnp.logical_not(is_owner))
    def _():
        gone(targets)


def shards(groups, blocks, activations, out_grads, proj_act, proj_out):
    tokens, depth = activations.shape
    examples = tokens // SEQ
    rank, span = proj_act.shape[1], proj_out.shape[1]
    devices, targets = groups * blocks, 2 * blocks
    group_ex, total_ex = examples * blocks, examples * devices
    ranks = rank // targets
    width = rank * span // blocks
    unit = total_ex // CHUNKS
    ex_c, rows_l = examples // CHUNKS, tokens // PARTS
    small = total_ex <= 1024
    slots = PARTS if small else AHEAD
    batch = groups // 2 if small else 1
    split = total_ex if small else 8
    vmem = pl.BlockSpec(memory_space=pltpu.VMEM)
    hbm = pl.BlockSpec(memory_space=pl.ANY)
    f32, low = jnp.float32, jnp.bfloat16
    dma = pltpu.SemaphoreType.DMA
    tiles = len(TILES)
    scores = pl.pallas_call(
        functools.partial(mix_kernel, groups, blocks, examples, ranks, width, slots, batch, small),
        out_shape=jax.ShapeDtypeStruct((examples, group_ex), f32),
        in_specs=[hbm] * 4,
        out_specs=vmem,
        scratch_shapes=[
            pltpu.VMEM((slots, rows_l, depth), low),
            pltpu.VMEM((slots, rows_l, depth), low),
            pltpu.VMEM((depth, rank), low),
            pltpu.VMEM((depth, span), low),
            pltpu.VMEM((span // 128, rank * ex_c, 128), f32),
            pltpu.VMEM((CHUNKS, targets, ranks, ex_c, span), low),
            pltpu.VMEM((ranks, total_ex, span), low),
            pltpu.VMEM((8, 128), f32),
            pltpu.VMEM((1, 128), f32),
            pltpu.VMEM((devices, 1, 128), f32),
            pltpu.VMEM((tiles, unit, unit), f32),
            pltpu.VMEM((total_ex, total_ex), f32),
            pltpu.VMEM((split, total_ex), low),
            pltpu.VMEM((split, total_ex), low),
            pltpu.VMEM((1, total_ex), f32),
            pltpu.VMEM((1, total_ex), f32),
            pltpu.VMEM((8, total_ex), f32),
            pltpu.VMEM((total_ex, 128), f32),
            pltpu.VMEM((batch * group_ex, total_ex), low),
            pltpu.VMEM((batch * group_ex, total_ex), low),
            pltpu.VMEM((batch * group_ex, total_ex), low),
            pltpu.VMEM((batch, ITERS, group_ex, group_ex), f32),
            pltpu.VMEM((groups // 2, group_ex, group_ex), f32),
            pltpu.VMEM((blocks, examples, group_ex), f32),
            dma((2 * slots,)), dma((2,)), dma((CHUNKS,)), dma((CHUNKS,)), dma, dma,
            dma((tiles,)), dma((tiles,)), dma, dma,
            dma((groups // 2 * blocks,)), dma((blocks,)),
        ],
        compiler_params=pltpu.CompilerParams(
            collective_id=0, has_side_effects=True,
            vmem_limit_bytes=(40 << 20) if small else 67043328,
        ),
    )(*[pltpu.with_memory_space_constraint(v, pltpu.HBM)
        for v in (activations, out_grads, proj_act, proj_out)])
    return scores * float(examples * groups)


def solution(mesh):
    in_specs = (P(("grp", "blk"), None), P(("grp", "blk"), None), P(), P())
    out_specs = P(("grp", "blk"), None)
    body = functools.partial(shards, mesh.shape["grp"], mesh.shape["blk"])
    return jax.shard_map(body, mesh=mesh, in_specs=in_specs, out_specs=out_specs, check_vma=False)
```
